256 devices in a mesh: row: 8 (over y, x_lo), col: 32 (over z, x_hi, core).
Axes of the slice: x: 4 (x_hi: 2, x_lo: 2; x = x_hi * 2 + x_lo), y: 4, z: 8, core: 2. Of those that a mesh axis runs over, the one named last changes fastest.
Arguments:
- observed: float32 [16, 1024, 4096], P(None, 'row', 'col'), may hold values from 0.2 to 3
- estimate: float32 [16, 1024, 4096], P(None, 'row', 'col'), may hold values from 0.5 to 2
- psf_bank: float32 [1024, 16, 2, 4, 33], P(('row', 'col')), may hold values from 0.05 to 1
- zone_ids: int32 [8, 32, 16, 2], P('row', 'col'), may hold values from 0 to 127, all different within a row
- mix_weights: float32 [8, 32, 16, 2], P('row', 'col'), may hold values from 0.2 to 1
- illumination: float32 [16, 128, 32], P(None, 'row', 'col'), may hold values from 0.3 to 3
Outputs:
- restored: float32 [16, 1024, 4096], P(None, 'row', 'col')
The draws below stay inside these ranges and needn't reach their ends.
Inputs may be any that keep to these rules, and one draw needn't show every extreme that they name: `zone_ids`: at each depth a tile names 2 different zones.
All inputs are finite; a program needn't handle non-finite values.
Results may differ from the reference program's by a relative error of at most 0.001.
Values may be sent and summed in bfloat16 or wider, within the bound.
A program may use at most 192 MiB of HBM per device.

```python
import math
import jax
import jax.numpy as jnp
from jax import lax

TR = 128
TC = 128
DEPTH = 16
TAPS = 33
RANK = 4
K = 2
CR = 16
ITERS = 2
NY = 1024
NX = 4096
ZBAND = 128
COARSE = 128
N_ROW = 8
N_COL = 32


def block_levels(rng, extent, pieces, smallest, top_value):
    loudness = 1.0
    for position, parts in pieces:
        steps = jax.random.uniform(jax.random.fold_in(jax.random.fold_in(rng, 6), position), (parts,), jnp.float32, smallest / len(pieces), top_value / len(pieces))
        loudness = loudness * jnp.repeat(jnp.exp(steps), extent[position] // parts).reshape((-1,) + (1,) * (len(extent) - 1 - position))
    return loudness


def different_ones(rng, rows, amount, top, lift):
    ranking = jax.random.permutation(jax.random.fold_in(rng, 1), amount)
    pull = ranking
    for power in range(3):
        pull = pull * pull // amount
    pull = pull * lift // amount
    lots = jax.random.randint(jax.random.fold_in(rng, 2), (rows, amount), 0, 4096) + pull
    holders = jax.random.permutation(jax.random.fold_in(rng, 3), rows)[jnp.arange(amount) % rows]
    lots = jnp.where(jnp.arange(rows)[:, None] == holders[None, :], 1 << 14, lots)
    score = lots * amount + jnp.arange(amount)
    return lax.top_k(score.astype(jnp.int32), top)[1].astype(jnp.int32)


def setup_inputs(seed: int = 0) -> dict:
    splits = jax.random.split(jax.random.key(seed), 7)
    return {
        "observed": jnp.clip(0.2 + 2.8 * jax.random.uniform(splits[0], (DEPTH, NY, NX), jnp.float32) ** block_levels(splits[0], (DEPTH, NY, NX), ((1, 8), (2, 32)), -0.2, 0.2), 0.2, 3.0),
        "estimate": jnp.clip(0.5 + 1.5 * jax.random.uniform(splits[1], (DEPTH, NY, NX), jnp.float32) ** block_levels(splits[1], (DEPTH, NY, NX), ((1, 8), (2, 32)), -0.2, 0.2), 0.5, 2.0),
        "psf_bank": jnp.clip(jnp.exp(math.log(1.0) - 2.9957323 * jax.random.uniform(splits[2], (N_ROW * ZBAND, DEPTH, 2, RANK, TAPS), jnp.float32) ** block_levels(splits[2], (N_ROW * ZBAND, DEPTH, 2, RANK, TAPS), ((0, 256),), -0.2, 0.2)), 0.05, 1.0),
        "zone_ids": different_ones(splits[3], N_ROW * N_COL * DEPTH, ZBAND, K, 256).reshape((N_ROW, N_COL, DEPTH, K)),
        "mix_weights": jnp.clip(jnp.exp(math.log(1.0) - 1.609438 * jax.random.uniform(splits[4], (N_ROW, N_COL, DEPTH, K), jnp.float32) ** block_levels(splits[4], (N_ROW, N_COL, DEPTH, K), ((0, 8), (1, 32)), -0.2, 0.2)), 0.2, 1.0),
        "illumination": jnp.clip(jnp.exp(math.log(3.0) - 2.3025851 * jax.random.uniform(splits[5], (DEPTH, COARSE, N_COL), jnp.float32) ** block_levels(splits[5], (DEPTH, COARSE, N_COL), ((1, 8), (2, 32)), -0.2, 0.2)), 0.3, 3.0),
    }


def band_table(size, taps):
    half = taps // 2
    offsets = jnp.arange(size + 2 * half, dtype=jnp.int32)[None, :] - jnp.arange(size, dtype=jnp.int32)[:, None]
    return (offsets[None, :, :] == jnp.arange(taps, dtype=jnp.int32)[:, None, None]).astype(jnp.float32)

def blur_tile(extended, row_taps, col_taps, table_rows, table_cols):
    rows_toe = jnp.einsum('zjt,tye->zjye', row_taps.astype(jnp.float32), table_rows, precision=lax.Precision.HIGHEST)
    cols_toe = jnp.einsum('zjt,txf->zjxf', col_taps.astype(jnp.float32), table_cols, precision=lax.Precision.HIGHEST)
    passes = jnp.einsum('zjye,zef->zjyf', rows_toe, extended, precision=lax.Precision.HIGHEST)
    passes = lax.optimization_barrier(passes.astype(jnp.bfloat16)).astype(jnp.float32)
    return jnp.einsum('zjyf,zjxf->zyx', passes, cols_toe, precision=lax.Precision.HIGHEST)

def whole_pass(field_b, row_taps, col_taps, table_rows, table_cols):
    half = TAPS // 2
    padded = jnp.pad(field_b.astype(jnp.float32), ((0, 0), (half, half), (half, half)))

    def one_tile(tile_index):
        band_row = tile_index // N_COL
        band_col = tile_index % N_COL
        extended = lax.dynamic_slice(padded, (jnp.int32(0), (band_row * TR).astype(jnp.int32), (band_col * TC).astype(jnp.int32)), (DEPTH, TR + 2 * half, TC + 2 * half))
        return blur_tile(extended, row_taps[band_row, band_col], col_taps[band_row, band_col], table_rows, table_cols)
    tiles = lax.map(one_tile, jnp.arange(N_ROW * N_COL, dtype=jnp.int32))
    tiles = tiles.reshape(N_ROW, N_COL, DEPTH, TR, TC).transpose(2, 0, 3, 1, 4)
    return tiles.reshape(DEPTH, N_ROW * TR, N_COL * TC)

def reference(observed, estimate, psf_bank, zone_ids, mix_weights, illumination):
    band = psf_bank.reshape(N_ROW, ZBAND, DEPTH, 2, RANK, TAPS)
    row_pick = jnp.arange(N_ROW, dtype=jnp.int32)[:, None, None, None]
    depth_pick = jnp.arange(DEPTH, dtype=jnp.int32)[None, None, :, None]
    selected = band[row_pick, zone_ids, depth_pick]
    row_f = selected[..., 0, :, :]
    col_f = selected[..., 1, :, :]
    total = jnp.sum(mix_weights[..., None] * jnp.sum(row_f, -1) * jnp.sum(col_f, -1), axis=(-2, -1))
    row_taps = (mix_weights[..., None, None] * row_f / total[..., None, None, None]).reshape(N_ROW, N_COL, DEPTH, K * RANK, TAPS).astype(jnp.bfloat16)
    col_taps = col_f.reshape(N_ROW, N_COL, DEPTH, K * RANK, TAPS).astype(jnp.bfloat16)
    back_rows = row_taps[..., ::-1]
    back_cols = col_taps[..., ::-1]
    table_rows = band_table(TR, TAPS)
    table_cols = band_table(TC, TAPS)
    length = COARSE
    stiffness = float(length * length) / 16.0
    main_diag = jnp.full((DEPTH, length), 1.0 + 2.0 * stiffness, jnp.float32)
    main_diag = main_diag.at[:, 0].set(1.0 + stiffness).at[:, -1].set(1.0 + stiffness)
    lower_diag = jnp.full((DEPTH, length), -stiffness, jnp.float32).at[:, 0].set(0.0)
    upper_diag = jnp.full((DEPTH, length), -stiffness, jnp.float32).at[:, -1].set(0.0)
    smooth = lax.linalg.tridiagonal_solve(lower_diag, main_diag, upper_diag, illumination)
    factor = jnp.repeat(jnp.repeat(smooth, TR // CR, axis=1), TC, axis=2)
    current = estimate
    for step in range(ITERS):
        blurred = whole_pass(current.astype(jnp.bfloat16), row_taps, col_taps, table_rows, table_cols)
        ratio = (observed / blurred).astype(jnp.bfloat16)
        back = whole_pass(ratio, back_rows, back_cols, table_rows, table_cols)
        current = current * back / factor
    return current
```

```python
import functools

import jax
import jax.numpy as jnp
import numpy as np
from jax import lax
from jax.experimental import pallas as pl
from jax.experimental.pallas import tpu as pltpu
from jax.sharding import PartitionSpec as P

MESH = pl.DeviceIdType.MESH
BF = jnp.bfloat16
F32 = jnp.float32
TAPS = 33
HALF = 16
GZ = 4
NT = (((1,), (1,)), ((), ()))


def mm(a, b):
    return jnp.dot(a, b, preferred_element_type=F32)


def mm_nt(a, b):
    return lax.dot_general(a, b, NT, preferred_element_type=F32)


def spread_table():
    w = np.zeros((128, 6 * 128), np.float32)
    for a in range(TAPS):
        plus, minus = (a - HALF) % 128, (HALF - a) % 128
        for lane in (a, TAPS + a):
            w[lane, minus] = 1.0
            w[lane, 128 + plus] = 1.0
            w[lane, 512:640] = 1.0
        w[2 * TAPS + a, 256 + plus] = 1.0
        w[2 * TAPS + a, 384 + minus] = 1.0
    w[3 * TAPS : 3 * TAPS + 3, 640:768] = 1.0
    return w.astype(BF)


def moves_table():
    eye = np.eye(128, dtype=np.float32)
    ends = np.concatenate([eye[:16], eye[112:]], 0)
    place = np.zeros((GZ, 128, 128), np.float32)
    sel_r = np.zeros((GZ * 16, 128), np.float32)
    sel_l = np.zeros((GZ * 16, 128), np.float32)
    for zz in range(GZ):
        for i in range(16):
            place[zz, i, zz * 32 + i] = 1.0
            place[zz, 112 + i, zz * 32 + 16 + i] = 1.0
            sel_r[zz * 16 + i, zz * 32 + i] = 1.0
            sel_l[zz * 16 + i, zz * 32 + 16 + i] = 1.0
    return np.concatenate([eye, ends, place.reshape(-1, 128), sel_r, sel_l], 0).astype(BF)


def smoothing_table(length, n_row, rows):
    stiff = float(length * length) / 16.0
    d = np.diff(np.eye(length), axis=0)
    inv = np.linalg.inv(np.eye(length) + stiff * d.T @ d)
    rep = np.repeat(inv, rows * n_row // length, axis=1)
    return rep.reshape(length, n_row, rows).transpose(1, 0, 2).astype(np.float32)


def kernel(
    n_row, n_col, obs, est, bank, ids, wts, ill_here, spread, moves, inv_all, out,
    ext, ystrip, strips, corn, cornsend, plane, ids_z, sel_send, sel_recv, ill, inv,
    base, rt, ctc, cth, ptc, pth, cur, obs_t, rfac,
    local_sem, psend, precv, isend, irecv, bsend, brecv, lsend, lrecv, hsend, hrecv,
):
    depth = obs.shape[0]
    groups = depth // GZ
    planes = n_col // 4
    row = lax.axis_index("row")
    col = lax.axis_index("col")
    zc = col // 4
    slot = lax.rem(col, 4)
    core_col = zc * 4 + slot + 1 - 2 * lax.rem(slot, 2)
    x_slot = lax.rem(slot + 2, 4)
    x_col = zc * 4 + x_slot

    def z_col(d):
        return lax.rem(zc + d + planes, planes) * 4 + slot

    up, down = lax.rem(row + n_row - 1, n_row), lax.rem(row + 1, n_row)
    left, right = lax.rem(col + n_col - 1, n_col), lax.rem(col + 1, n_col)

    inv_copy = pltpu.make_async_copy(inv_all.at[row], inv, local_sem)
    inv_copy.start()

    for p in range(4):
        ext[p, :, 128:160, :] = jnp.zeros((depth, 32, 256), BF)
    ystrip[...] = jnp.zeros_like(ystrip)
    corn[...] = jnp.zeros_like(corn)

    barrier = pltpu.get_barrier_semaphore()
    friends = [(row, z_col(d)) for d in range(1, planes)]
    friends += [(row, core_col), (row, x_col)]
    friends += [(lax.rem(row + d, n_row), col) for d in range(1, n_row)]
    friends += [(row, left), (row, right)]
    friends += [(up, left), (up, right), (down, left), (down, right)]
    for friend in friends:
        pl.semaphore_signal(barrier, inc=1, device_id=friend, device_id_type=MESH)
    pl.semaphore_wait(barrier, len(friends))

    def remote(src, dst, s, r, to):
        return pltpu.make_async_remote_copy(
            src_ref=src, dst_ref=dst, send_sem=s, recv_sem=r, device_id=to, device_id_type=MESH
        )

    x_copy = remote(bank, plane.at[slot], psend.at[0], precv.at[0], (row, x_col))
    core_copy = remote(bank, plane.at[slot], psend.at[1], precv.at[1], (row, core_col))
    x_copy.start()
    core_copy.start()
    id_copies = [
        remote(ids, ids_z.at[d], isend.at[d], irecv.at[d], (row, z_col(-d))) for d in range(1, planes)
    ]
    for c in id_copies:
        c.start()
    ill_copies = [
        remote(
            ill_here, ill.at[pl.ds(row * 16, 16)], lsend.at[d], lrecv.at[d], (lax.rem(row + d, n_row), col)
        )
        for d in range(1, n_row)
    ]
    for c in ill_copies:
        c.start()
    plane[slot] = bank[...]
    ids_z[0] = ids[...]
    ill[pl.ds(row * 16, 16)] = ill_here[...]

    has = {"u": row > 0, "d": row < n_row - 1, "l": col > 0, "r": col < n_col - 1}

    def halo_copies(p, g):
        zs = pl.ds(g * GZ, GZ)
        top, bottom = pl.ds(0, 16), pl.ds(16, 16)
        mid = pl.ds(0, 128)
        plan = [
            ("l", ext.at[p, zs, pl.ds(0, 16), mid], ext.at[p, zs, pl.ds(128, 16), mid], (row, left)),
            ("r", ext.at[p, zs, pl.ds(112, 16), mid], ext.at[p, zs, pl.ds(144, 16), mid], (row, right)),
            ("u", strips.at[p, zs, top], ystrip.at[p, zs, top], (up, col)),
            ("d", strips.at[p, zs, bottom], ystrip.at[p, zs, bottom], (down, col)),
            ("ul", cornsend.at[p, g, top], corn.at[p, g, 0, top], (up, left)),
            ("dl", cornsend.at[p, g, bottom], corn.at[p, g, 0, bottom], (down, left)),
            ("ur", cornsend.at[p, g, top], corn.at[p, g, 1, top], (up, right)),
            ("dr", cornsend.at[p, g, bottom], corn.at[p, g, 1, bottom], (down, right)),
        ]
        return [
            (where, remote(src, dst, hsend.at[p, g, i], hrecv.at[p, g, i], to))
            for i, (where, src, dst, to) in enumerate(plan)
        ]

    opposite = {"u": "d", "d": "u", "l": "r", "r": "l"}

    def there(where):
        ok = has[where[0]]
        for w in where[1:]:
            ok = jnp.logical_and(ok, has[w])
        return ok

    def halo_start(p, g):
        for where, c in halo_copies(p, g):
            @pl.when(there(where))
            def _():
                c.start()

    def halo_wait_recv(p, g):
        for where, c in halo_copies(p, g):
            @pl.when(there("".join(opposite[w] for w in where)))
            def _():
                c.wait_recv()

    def halo_wait_send(p, g):
        for where, c in halo_copies(p, g):
            @pl.when(there(where))
            def _():
                c.wait_send()

    def place_at(zz):
        return moves[160 + zz * 128 : 288 + zz * 128]

    def strip_of(p, z, field_b):
        ext[p, z, 0:128, 0:128] = field_b
        s = mm_nt(moves[128:160], field_b).astype(BF)
        strips[p, z] = s
        return s

    @pl.loop(0, groups)
    def _(g):
        acc = jnp.zeros((32, 128), F32)
        for zz in range(GZ):
            z = g * GZ + zz
            c = jnp.transpose(est[z])
            cur[z] = c
            obs_t[z] = jnp.transpose(obs[z])
            acc = acc + mm(strip_of(0, z, c.astype(BF)), place_at(zz))
        cornsend[0, g] = acc.astype(BF)
        halo_start(0, g)

    x_copy.wait_recv()
    forward = remote(plane.at[x_slot], plane.at[x_slot], psend.at[2], precv.at[2], (row, core_col))
    forward.start()
    core_copy.wait_recv()
    for c in id_copies:
        c.wait_recv()
    forward.wait_recv()

    def selection(d):
        for k in range(2):
            mine = ids_z[d, k].astype(F32)
            picked = [jnp.zeros((depth, 128), F32) for _ in range(4)]
            for s in range(4):
                for i in range(4):
                    zone = (zc * 16 + s * 4 + i).astype(F32)
                    hit = mine == zone
                    for q in range(4):
                        picked[q] = jnp.where(hit, plane[s, i, q].astype(F32), picked[q])
            for q in range(4):
                sel_send[d, k * 4 + q] = picked[q].astype(BF)

    sel_copies = [
        remote(sel_send.at[d], sel_recv.at[d], bsend.at[d], brecv.at[d], (row, z_col(d)))
        for d in range(1, planes)
    ]
    for d in range(1, planes):
        selection(d)
        sel_copies[d - 1].start()
    selection(0)

    inv_copy.wait()
    for c in ill_copies:
        c.wait_recv()
    fac = jnp.dot(
        jnp.transpose(ill[...])[0:depth], inv[...], precision=lax.Precision.HIGHEST,
        preferred_element_type=F32,
    )
    rfac[...] = 1.0 / fac

    for c in sel_copies:
        c.wait_recv()
    total = jnp.zeros((depth, 128), F32)
    for j in range(8):
        s = sel_send[0, j].astype(F32)
        for d in range(1, planes):
            s = s + sel_recv[d, j].astype(F32)
        b = mm(s.astype(BF), spread[...])
        total = total + wts[j // 4] * b[:, 512:640] * b[:, 640:768]
        for t in range(4):
            base[t, j] = b[:, t * 128 : (t + 1) * 128]
    for j in range(8):
        for t in range(2):
            base[t, j] = (wts[j // 4] * base[t, j]) / total

    lanes = lax.broadcasted_iota(jnp.int32, (16, 128), 1)
    low = lanes < 64

    def circulant(t, j, z):
        b = jnp.broadcast_to(base[t, j, pl.ds(z, 1), :], (128, 128))
        return pltpu.roll(b, 0, 1, stride=1, stride_axis=0)

    def build(way, z):
        zero = jnp.zeros((16, 128), F32)
        left_h = [zero, zero]
        right_h = [zero, zero]
        for j in range(8):
            js = slice(j * 128, (j + 1) * 128)
            r = circulant(way, j, z)
            first, last = r[0:16], r[112:128]
            rt[way, z, 0:16, js] = jnp.where(low, first, 0.0).astype(BF)
            rt[way, z, 16:112, js] = r[16:112].astype(BF)
            rt[way, z, 112:128, js] = jnp.where(low, 0.0, last).astype(BF)
            rt[way, z, 128:144, js] = jnp.where(low, 0.0, first).astype(BF)
            rt[way, z, 144:160, js] = jnp.where(low, last, 0.0).astype(BF)
            c = circulant(2 + way, j, z)
            first, last = c[0:16], c[112:128]
            ctc[way, z, 0:16, js] = jnp.where(low, first, 0.0).astype(BF)
            ctc[way, z, 16:112, js] = c[16:112].astype(BF)
            ctc[way, z, 112:128, js] = jnp.where(low, 0.0, last).astype(BF)
            at = (j % 4) * 32
            left_h[j // 4] += pltpu.roll(jnp.where(low, 0.0, first), (at + 16 + 16) % 128, 1)
            right_h[j // 4] += pltpu.roll(jnp.where(low, last, 0.0), at, 1)
        for h in range(2):
            hs = slice(h * 128, (h + 1) * 128)
            cth[way, z, 0:16, hs] = left_h[h].astype(BF)
            cth[way, z, 16:112, hs] = jnp.zeros((96, 128), BF)
            cth[way, z, 112:128, hs] = right_h[h].astype(BF)

    def blur(p, z, zz, corner_r, corner_l):
        way = p % 2
        ext[p, z, 0:128, 128:160] = mm_nt(moves[0:128], ystrip[p, z]).astype(BF)
        ext[p, z, 128:144, 128:160] = corner_r[zz * 16 : zz * 16 + 16]
        ext[p, z, 144:160, 128:160] = corner_l[zz * 16 : zz * 16 + 16]
        field = ext[p, z, :, 0:160]
        for jp in range(4):
            o = mm(field, rt[way, z, :, jp * 256 : (jp + 1) * 256]).astype(BF)
            for h in range(2):
                j = jp * 2 + h
                ptc[zz, j * 128 : (j + 1) * 128] = o[0:128, h * 128 : (h + 1) * 128]
                pth[zz, j * 32 : (j + 1) * 32] = o[128:160, h * 128 : (h + 1) * 128]
        return mm(ctc[way, z], ptc[zz]) + mm(cth[way, z], pth[zz])

    first_sel = 160 + GZ * 128
    for p in range(4):
        @pl.loop(0, groups)
        def _(g):
            if p < 2:
                @pl.loop(0, GZ)
                def _(zz):
                    build(p, g * GZ + zz)
            halo_wait_recv(p, g)
            corner_r = mm_nt(moves[first_sel : first_sel + GZ * 16], corn[p, g, 0]).astype(BF)
            corner_l = mm_nt(moves[first_sel + GZ * 16 : first_sel + 2 * GZ * 16], corn[p, g, 1]).astype(BF)
            acc = jnp.zeros((32, 128), F32)
            for zz in range(GZ):
                z = g * GZ + zz
                f = blur(p, z, zz, corner_r, corner_l)
                if p % 2 == 0:
                    field = (obs_t[z] / f).astype(BF)
                else:
                    new = cur[z] * f * rfac[pl.ds(z, 1), :]
                    if p == 3:
                        out[z] = jnp.transpose(new)
                        continue
                    cur[z] = new
                    field = new.astype(BF)
                acc = acc + mm(strip_of(p + 1, z, field), place_at(zz))
            if p < 3:
                cornsend[p + 1, g] = acc.astype(BF)
                halo_start(p + 1, g)

    x_copy.wait_send()
    core_copy.wait_send()
    forward.wait_send()
    for c in id_copies + ill_copies + sel_copies:
        c.wait_send()
    for p in range(4):
        @pl.loop(0, groups)
        def _(g):
            halo_wait_send(p, g)


def shards(n_row, n_col, observed, estimate, psf_bank, zone_ids, mix_weights, illumination):
    depth, rows, cols = estimate.shape
    zones = psf_bank.shape[0]
    groups = depth // GZ
    planes = n_col // 4
    cells = psf_bank.transpose(2, 0, 3, 1, 4)
    row_f, col_f = cells[0], cells[1]

    def high(v):
        return lax.reduce_precision(v, 8, 7)

    sums = jnp.sum(col_f, -1, keepdims=True)
    r_hi = high(row_f)
    s_hi = high(sums)
    s_mid = high(sums - s_hi)
    bank = jnp.concatenate(
        [r_hi, row_f - r_hi, col_f, s_hi, s_mid, sums - s_hi - s_mid,
         jnp.zeros((zones, 4, depth, 128 - 3 * TAPS - 3), F32)], -1,
    ).astype(BF)
    ids = jnp.broadcast_to(zone_ids[0, 0].T[:, :, None], (2, depth, 128)).astype(BF)
    wts = jnp.broadcast_to(mix_weights[0, 0].T[:, :, None], (2, depth, 128))
    ill_here = jnp.pad(illumination[:, :, 0].T, ((0, 0), (0, 128 - depth)))
    length = illumination.shape[1] * n_row
    spread = jnp.asarray(spread_table())
    moves = jnp.asarray(moves_table())
    inv_all = jnp.asarray(smoothing_table(length, n_row, rows))
    vmem = pl.BlockSpec(memory_space=pltpu.VMEM)
    dma = pltpu.SemaphoreType.DMA
    return pl.pallas_call(
        functools.partial(kernel, n_row, n_col),
        out_shape=jax.ShapeDtypeStruct(estimate.shape, F32),
        in_specs=[vmem] * 8 + [pl.BlockSpec(memory_space=pl.ANY)],
        out_specs=vmem,
        scratch_shapes=[
            pltpu.VMEM((4, depth, 160, 256), BF),
            pltpu.VMEM((4, depth, 32, 128), BF),
            pltpu.VMEM((4, depth, 32, 128), BF),
            pltpu.VMEM((4, groups, 2, 32, 128), BF),
            pltpu.VMEM((4, groups, 32, 128), BF),
            pltpu.VMEM((4, zones, 4, depth, 128), BF),
            pltpu.VMEM((planes, 2, depth, 128), BF),
            pltpu.VMEM((planes, 8, depth, 128), BF),
            pltpu.VMEM((planes, 8, depth, 128), BF),
            pltpu.VMEM((length, 128), F32),
            pltpu.VMEM((length, rows), F32),
            pltpu.VMEM((4, 8, depth, 128), F32),
            pltpu.VMEM((2, depth, 160, 1024), BF),
            pltpu.VMEM((2, depth, 128, 1024), BF),
            pltpu.VMEM((2, depth, 128, 256), BF),
            pltpu.VMEM((GZ, 1024, 128), BF),
            pltpu.VMEM((GZ, 256, 128), BF),
            pltpu.VMEM((depth, 128, 128), F32),
            pltpu.VMEM((depth, 128, 128), F32),
            pltpu.VMEM((depth, 128), F32),
            dma,
            dma((3,)), dma((3,)),
            dma((planes,)), dma((planes,)),
            dma((planes,)), dma((planes,)),
            dma((n_row,)), dma((n_row,)),
            dma((4, groups, 8)), dma((4, groups, 8)),
        ],
        compiler_params=pltpu.CompilerParams(
            collective_id=0, has_side_effects=True, vmem_limit_bytes=60 * 2**20
        ),
        name="deconvolve",
    )(observed, estimate, bank, ids, wts, ill_here, spread, moves, inv_all)


def solution(mesh):
    placed = (
        P(None, "row", "col"),
        P(None, "row", "col"),
        P(("row", "col"), None, None, None, None),
        P("row", "col", None, None),
        P("row", "col", None, None),
        P(None, "row", "col"),
    )
    return jax.shard_map(
        functools.partial(shards, mesh.shape["row"], mesh.shape["col"]),
        mesh=mesh, in_specs=placed, out_specs=P(None, "row", "col"), check_vma=False,
    )
```

```python
import functools

import jax
import jax.numpy as jnp
import numpy as np
from jax import lax
from jax.experimental import pallas as pl
from jax.experimental.pallas import tpu as pltpu
from jax.sharding import PartitionSpec as P

MESH = pl.DeviceIdType.MESH
BF = jnp.bfloat16
F32 = jnp.float32
TAPS = 33
HALF = 16
GZ = 4
NT = (((1,), (1,)), ((), ()))


def mm(a, b):
    return jnp.dot(a, b, preferred_element_type=F32)


def mm_nt(a, b):
    return lax.dot_general(a, b, NT, preferred_element_type=F32)


def spread_table():
    w = np.zeros((128, 6 * 128), np.float32)
    for a in range(TAPS):
        plus, minus = (a - HALF) % 128, (HALF - a) % 128
        for lane in (a, TAPS + a):
            w[lane, minus] = 1.0
            w[lane, 128 + plus] = 1.0
            w[lane, 512:640] = 1.0
        w[2 * TAPS + a, 256 + plus] = 1.0
        w[2 * TAPS + a, 384 + minus] = 1.0
    w[3 * TAPS : 3 * TAPS + 3, 640:768] = 1.0
    return w.astype(BF)


def moves_table():
    eye = np.eye(128, dtype=np.float32)
    ends = np.concatenate([eye[:16], eye[112:]], 0)
    sel_r = np.zeros((GZ * 16, 128), np.float32)
    sel_l = np.zeros((GZ * 16, 128), np.float32)
    for zz in range(GZ):
        for i in range(16):
            sel_l[zz * 16 + i, zz * 32 + i] = 1.0
            sel_r[zz * 16 + i, zz * 32 + 16 + i] = 1.0
    none = np.zeros_like(sel_r)
    sel = np.block([[sel_r, none], [none, sel_l]])
    return np.concatenate([eye, ends], 0).astype(BF), sel.astype(BF)


def smoothing_table(length, n_row, rows):
    stiff = float(length * length) / 16.0
    d = np.diff(np.eye(length), axis=0)
    inv = np.linalg.inv(np.eye(length) + stiff * d.T @ d)
    rep = np.repeat(inv, rows * n_row // length, axis=1)
    return rep.reshape(length, n_row, rows).transpose(1, 0, 2).astype(np.float32)


def kernel(
    n_row, n_col, cells, ids_in, wts_in, ill_in, spread, moves, picks, obs_hbm, est_hbm, inv_all, out_hbm,
    obs, est, out, wide, bank, ids, wts, ill_here, ext0, ext1, ext2, ext3, ystrip, strips, corn, cornsend, plane, ids_z, sel_send, sel_recv, ill, inv,
    base, rt0, rt1, ctc0, ctc1, cth0, cth1, ptc, pth, cur, obs_t, rfac,
    local_sem, est_sem, obs_sem, out_sem, psend, precv, isend, irecv, bsend, brecv, lsend, lrecv, hsend, hrecv,
):
    ext = (ext0, ext1, ext2, ext3)
    rt, ctc, cth = (rt0, rt1), (ctc0, ctc1), (cth0, cth1)
    depth = obs.shape[0]
    groups = depth // GZ
    planes = n_col // 4
    row = lax.axis_index("row")
    col = lax.axis_index("col")
    zc = col // 4
    slot = lax.rem(col, 4)
    core_col = zc * 4 + slot + 1 - 2 * lax.rem(slot, 2)
    x_slot = lax.rem(slot + 2, 4)
    x_col = zc * 4 + x_slot

    def z_col(d):
        return lax.rem(zc + d + planes, planes) * 4 + slot

    up, down = lax.rem(row + n_row - 1, n_row), lax.rem(row + 1, n_row)
    left, right = lax.rem(col + n_col - 1, n_col), lax.rem(col + 1, n_col)

    inv_copy = pltpu.make_async_copy(inv_all.at[row], inv, local_sem)
    inv_copy.start()
    est_copy = pltpu.make_async_copy(est_hbm, est, est_sem)
    est_copy.start()
    obs_copy = pltpu.make_async_copy(obs_hbm, obs, obs_sem)
    obs_copy.start()
    zones = cells.shape[1]
    lane = lax.broadcasted_iota(jnp.int32, (depth, 128), 1)
    wide[...] = jnp.zeros_like(wide)
    wide[:, :, :, :, 0:TAPS] = cells[...]
    for i in range(zones):
        for q in range(4):
            r, c = wide[0, i, q], wide[1, i, q]
            r_hi = r.astype(BF).astype(F32)
            total_c = jnp.sum(c, -1, keepdims=True)
            s_hi = total_c.astype(BF).astype(F32)
            s_mid = (total_c - s_hi).astype(BF).astype(F32)
            packed = r_hi + pltpu.roll(r - r_hi, TAPS, 1) + pltpu.roll(c, 2 * TAPS, 1)
            packed = jnp.where(lane == 3 * TAPS, s_hi, packed)
            packed = jnp.where(lane == 3 * TAPS + 1, s_mid, packed)
            packed = jnp.where(lane == 3 * TAPS + 2, total_c - s_hi - s_mid, packed)
            bank[i, q] = packed.astype(BF)
    for k in range(2):
        ids[k] = jnp.transpose(jnp.broadcast_to(ids_in[k : k + 1].astype(F32), (128, depth))).astype(BF)
        wts[k] = jnp.transpose(jnp.broadcast_to(wts_in[k : k + 1], (128, depth)))
    ill_here[...] = jnp.zeros_like(ill_here)
    ill_here[:, 0 : ill_in.shape[1]] = ill_in[...]

    for p in range(4):
        ext[p][:, 128:160, :] = jnp.zeros((depth, 32, 256), BF)
    ystrip[...] = jnp.zeros_like(ystrip)
    corn[...] = jnp.zeros_like(corn)

    barrier = pltpu.get_barrier_semaphore()
    friends = [(row, z_col(d)) for d in range(1, planes)]
    friends += [(row, core_col), (row, x_col)]
    friends += [(lax.rem(row + d, n_row), col) for d in range(1, n_row)]
    friends += [(row, left), (row, right)]
    friends += [(up, left), (up, right), (down, left), (down, right)]
    for friend in friends:
        pl.semaphore_signal(barrier, inc=1, device_id=friend, device_id_type=MESH)
    pl.semaphore_wait(barrier, len(friends))

    def remote(src, dst, s, r, to):
        return pltpu.make_async_remote_copy(
            src_ref=src, dst_ref=dst, send_sem=s, recv_sem=r, device_id=to, device_id_type=MESH
        )

    x_copy = remote(bank, plane.at[slot], psend.at[0], precv.at[0], (row, x_col))
    core_copy = remote(bank, plane.at[slot], psend.at[1], precv.at[1], (row, core_col))
    x_copy.start()
    core_copy.start()
    id_copies = [
        remote(ids, ids_z.at[d], isend.at[d], irecv.at[d], (row, z_col(-d))) for d in range(1, planes)
    ]
    for c in id_copies:
        c.start()
    ill_copies = [
        remote(
            ill_here, ill.at[row], lsend.at[d], lrecv.at[d], (lax.rem(row + d, n_row), col)
        )
        for d in range(1, n_row)
    ]
    for c in ill_copies:
        c.start()
    plane[slot] = bank[...]
    ids_z[0] = ids[...]
    ill[row] = ill_here[...]

    has = {"u": row > 0, "d": row < n_row - 1, "l": col > 0, "r": col < n_col - 1}

    def halo_copies(p, g):
        zs = pl.ds(g * GZ, GZ)
        top, bottom = pl.ds(0, 16), pl.ds(16, 16)
        mid = pl.ds(0, 128)
        plan = [
            ("l", ext[p].at[zs, pl.ds(0, 16), mid], ext[p].at[zs, pl.ds(128, 16), mid], (row, left)),
            ("r", ext[p].at[zs, pl.ds(112, 16), mid], ext[p].at[zs, pl.ds(144, 16), mid], (row, right)),
            ("u", strips.at[p, zs, top], ystrip.at[p, zs, top], (up, col)),
            ("d", strips.at[p, zs, bottom], ystrip.at[p, zs, bottom], (down, col)),
            ("ul", cornsend.at[p, g, top], corn.at[p, g, top, pl.ds(0, 128)], (up, left)),
            ("dl", cornsend.at[p, g, bottom], corn.at[p, g, bottom, pl.ds(0, 128)], (down, left)),
            ("ur", cornsend.at[p, g, top], corn.at[p, g, top, pl.ds(128, 128)], (up, right)),
            ("dr", cornsend.at[p, g, bottom], corn.at[p, g, bottom, pl.ds(128, 128)], (down, right)),
        ]
        return [
            (where, remote(src, dst, hsend.at[p, g, i], hrecv.at[p, g, i], to))
            for i, (where, src, dst, to) in enumerate(plan)
        ]

    opposite = {"u": "d", "d": "u", "l": "r", "r": "l"}

    def there(where):
        ok = has[where[0]]
        for w in where[1:]:
            ok = jnp.logical_and(ok, has[w])
        return ok

    def halo_start(p, g):
        for where, c in halo_copies(p, g):
            @pl.when(there(where))
            def _():
                c.start()

    def halo_wait_recv(p, g):
        for where, c in halo_copies(p, g):
            @pl.when(there("".join(opposite[w] for w in where)))
            def _():
                c.wait_recv()

    def halo_wait_send(p, g):
        for where, c in halo_copies(p, g):
            @pl.when(there(where))
            def _():
                c.wait_send()

    quarter = lax.broadcasted_iota(jnp.int32, (32, 128), 1) // 32

    def pack(p, g, fields):
        for zz in range(GZ):
            ext[p][g * GZ + zz, 0:128, 0:128] = fields[zz]
        s = mm_nt(moves[128:160], jnp.concatenate(fields, 0)).astype(BF)
        for zz in range(GZ):
            strips[p, g * GZ + zz] = s[:, zz * 128 : (zz + 1) * 128]
        c = jnp.zeros((32, 128), F32)
        for zz in range(GZ):
            turned = pltpu.roll(s[:, zz * 128 : (zz + 1) * 128].astype(F32), 16 + zz * 32, 1)
            c = jnp.where(quarter == zz, turned, c)
        cornsend[p, g] = c.astype(BF)
        halo_start(p, g)

    est_copy.wait()

    @pl.loop(0, groups)
    def _(g):
        fields = []
        for zz in range(GZ):
            z = g * GZ + zz
            c = jnp.transpose(est[z])
            cur[z] = c
            fields.append(c.astype(BF))
        pack(0, g, fields)

    x_copy.wait_recv()
    forward = remote(plane.at[x_slot], plane.at[x_slot], psend.at[2], precv.at[2], (row, core_col))
    forward.start()
    core_copy.wait_recv()
    for c in id_copies:
        c.wait_recv()
    forward.wait_recv()

    def selection(d):
        for k in range(2):
            mine = ids_z[d, k].astype(F32)
            picked = [jnp.zeros((depth, 128), F32) for _ in range(4)]
            for s in range(4):
                for i in range(4):
                    zone = (zc * 16 + s * 4 + i).astype(F32)
                    hit = mine == zone
                    for q in range(4):
                        picked[q] = jnp.where(hit, plane[s, i, q].astype(F32), picked[q])
            for q in range(4):
                sel_send[d, k * 4 + q] = picked[q].astype(BF)

    sel_copies = [
        remote(sel_send.at[d], sel_recv.at[d], bsend.at[d], brecv.at[d], (row, z_col(d)))
        for d in range(1, planes)
    ]
    for d in range(1, planes):
        selection(d)
        sel_copies[d - 1].start()
    selection(0)

    inv_copy.wait()
    for c in ill_copies:
        c.wait_recv()
    coarse = ill_in.shape[1]
    fac = jnp.zeros((depth, inv.shape[1]), F32)
    for i in range(n_row):
        fac = fac + jnp.dot(
            ill[i, :, 0:coarse], inv[i * coarse : (i + 1) * coarse],
            precision=lax.Precision.HIGHEST, preferred_element_type=F32,
        )
    rfac[...] = 1.0 / fac

    obs_copy.wait()
    for c in sel_copies:
        c.wait_recv()
    picked = sel_send[0].astype(F32)
    for d in range(1, planes):
        picked = picked + sel_recv[d].astype(F32)
    b = mm(jnp.reshape(picked, (8 * depth, 128)).astype(BF), spread[...])
    total = jnp.zeros((depth, 128), F32)
    for j in range(8):
        r = b[j * depth : (j + 1) * depth]
        total = total + wts[j // 4] * r[:, 512:640] * r[:, 640:768]
    for j in range(8):
        r = b[j * depth : (j + 1) * depth]
        for t in range(4):
            v = r[:, t * 128 : (t + 1) * 128]
            base[t, j] = (wts[j // 4] * v) / total if t < 2 else v

    low = lax.broadcasted_iota(jnp.int32, (16, 128), 1) < 64
    lower = low.astype(F32).astype(BF)
    upper = 1.0 - lower

    def circulant(t, j, z):
        b = jnp.broadcast_to(base[t, j, pl.ds(z, 1), :], (16, 128))
        b = pltpu.roll(b, 0, 1, stride=1, stride_axis=0).astype(BF)
        return [pltpu.roll(b, 16 * i, 1) if i else b for i in range(8)]

    def build(way, z):
        left_h = [0.0, 0.0]
        right_h = [0.0, 0.0]
        for j in range(8):
            js = slice(j * 128, (j + 1) * 128)
            r = circulant(way, j, z)
            c = circulant(2 + way, j, z)
            for i in range(1, 7):
                rt[way][z, i * 16 : i * 16 + 16, js] = r[i]
                ctc[way][z, i * 16 : i * 16 + 16, js] = c[i]
            rt[way][z, 0:16, js] = r[0] * lower
            rt[way][z, 112:128, js] = r[7] * upper
            rt[way][z, 128:144, js] = r[0] * upper
            rt[way][z, 144:160, js] = r[7] * lower
            ctc[way][z, 0:16, js] = c[0] * lower
            ctc[way][z, 112:128, js] = c[7] * upper
            at = (j % 4) * 32
            left_h[j // 4] += pltpu.roll(c[0] * upper, (at + 16 + 16) % 128, 1)
            right_h[j // 4] += pltpu.roll(c[7] * lower, at, 1) if at else c[7] * lower
        for h in range(2):
            hs = slice(h * 128, (h + 1) * 128)
            cth[way][z, 0:16, hs] = left_h[h]
            cth[way][z, 16:112, hs] = jnp.zeros((96, 128), BF)
            cth[way][z, 112:128, hs] = right_h[h]

    def out_copy(g):
        zs = pl.ds(g * GZ, GZ)
        return pltpu.make_async_copy(out.at[zs], out_hbm.at[zs], out_sem.at[g])

    def unpack(p, g):
        edges = jnp.reshape(ystrip[p, pl.ds(g * GZ, GZ)], (GZ * 32, 128))
        mid = mm_nt(moves[0:128], edges)
        corner = mm_nt(picks[...], corn[p, g]).astype(BF)
        for zz in range(GZ):
            z = g * GZ + zz
            turned = pltpu.roll(mid, 128 - zz * 32, 1) if zz else mid
            ext[p][z, 0:128, 128:160] = turned[:, 0:32].astype(BF)
            at = zz * 16
            ext[p][z, 128:144, 128:160] = corner[at : at + 16]
            at = (GZ + zz) * 16
            ext[p][z, 144:160, 128:160] = corner[at : at + 16]

    def rows_stage(p, z, zz):
        field = ext[p][z, :, 0:160]
        for jp in range(4):
            o = mm(field, rt[p % 2][z, :, jp * 256 : (jp + 1) * 256]).astype(BF)
            for h in range(2):
                j = jp * 2 + h
                ptc[zz, j * 128 : (j + 1) * 128] = o[0:128, h * 128 : (h + 1) * 128]
                pth[zz, j * 32 : (j + 1) * 32] = o[128:160, h * 128 : (h + 1) * 128]

    def cols_stage(p, z, zz):
        return mm(ctc[p % 2][z], ptc[zz]) + mm(cth[p % 2][z], pth[zz])

    for p in range(4):
        @pl.loop(0, groups)
        def _(g):
            if p < 2:
                @pl.loop(0, GZ)
                def _(zz):
                    build(p, g * GZ + zz)
            halo_wait_recv(p, g)
            unpack(p, g)
            fields = []
            for step in range(GZ + 1):
                if step < GZ:
                    rows_stage(p, g * GZ + step, step)
                if step == 0:
                    continue
                zz = step - 1
                z = g * GZ + zz
                f = cols_stage(p, z, zz)
                if p % 2 == 0:
                    fields.append((jnp.transpose(obs[z]) / f if p == 0 else obs_t[z] / f).astype(BF))
                    if p == 0:
                        obs_t[z] = jnp.transpose(obs[z])
                else:
                    new = cur[z] * f * rfac[pl.ds(z, 1), :]
                    if p == 3:
                        out[z] = jnp.transpose(new)
                    else:
                        cur[z] = new
                        fields.append(new.astype(BF))
            if p < 3:
                pack(p + 1, g, fields)
            else:
                out_copy(g).start()

    x_copy.wait_send()
    core_copy.wait_send()
    forward.wait_send()
    for c in id_copies + ill_copies + sel_copies:
        c.wait_send()
    for g in range(groups):
        out_copy(g).wait()
    for p in range(4):
        @pl.loop(0, groups)
        def _(g):
            halo_wait_send(p, g)


def shards(n_row, n_col, observed, estimate, psf_bank, zone_ids, mix_weights, illumination):
    depth, rows, cols = estimate.shape
    zones = psf_bank.shape[0]
    groups = depth // GZ
    planes = n_col // 4
    cells = psf_bank.transpose(2, 0, 3, 1, 4)
    ids = zone_ids[0, 0].T
    wts = mix_weights[0, 0].T
    ill_here = illumination[:, :, 0]
    length = illumination.shape[1] * n_row
    spread = jnp.asarray(spread_table())
    moves, picks = map(jnp.asarray, moves_table())
    inv_all = jnp.asarray(smoothing_table(length, n_row, rows))
    vmem = pl.BlockSpec(memory_space=pltpu.VMEM)
    hbm = pl.BlockSpec(memory_space=pl.ANY)
    dma = pltpu.SemaphoreType.DMA
    return pl.pallas_call(
        functools.partial(kernel, n_row, n_col),
        out_shape=jax.ShapeDtypeStruct(estimate.shape, F32),
        in_specs=[vmem] * 7 + [hbm] * 3,
        out_specs=hbm,
        scratch_shapes=[
            *[pltpu.VMEM((depth, rows, cols), F32)] * 3,
            pltpu.VMEM((2, zones, 4, depth, 128), F32),
            pltpu.VMEM((zones, 4, depth, 128), BF),
            pltpu.VMEM((2, depth, 128), BF),
            pltpu.VMEM((2, depth, 128), F32),
            pltpu.VMEM((depth, 128), F32),
            *[pltpu.VMEM((depth, 160, 256), BF)] * 4,
            pltpu.VMEM((4, depth, 32, 128), BF),
            pltpu.VMEM((4, depth, 32, 128), BF),
            pltpu.VMEM((4, groups, 32, 256), BF),
            pltpu.VMEM((4, groups, 32, 128), BF),
            pltpu.VMEM((4, zones, 4, depth, 128), BF),
            pltpu.VMEM((planes, 2, depth, 128), BF),
            pltpu.VMEM((planes, 8, depth, 128), BF),
            pltpu.VMEM((planes, 8, depth, 128), BF),
            pltpu.VMEM((n_row, depth, 128), F32),
            pltpu.VMEM((length, rows), F32),
            pltpu.VMEM((4, 8, depth, 128), F32),
            *[pltpu.VMEM((depth, 160, 1024), BF)] * 2,
            *[pltpu.VMEM((depth, 128, 1024), BF)] * 2,
            *[pltpu.VMEM((depth, 128, 256), BF)] * 2,
            pltpu.VMEM((GZ, 1024, 128), BF),
            pltpu.VMEM((GZ, 256, 128), BF),
            pltpu.VMEM((depth, 128, 128), F32),
            pltpu.VMEM((depth, 128, 128), F32),
            pltpu.VMEM((depth, 128), F32),
            dma, dma, dma, dma((groups,)),
            dma((3,)), dma((3,)),
            dma((planes,)), dma((planes,)),
            dma((planes,)), dma((planes,)),
            dma((n_row,)), dma((n_row,)),
            dma((4, groups, 8)), dma((4, groups, 8)),
        ],
        compiler_params=pltpu.CompilerParams(
            collective_id=0, has_side_effects=True, vmem_limit_bytes=60 * 2**20
        ),
        name="deconvolve",
    )(cells, ids, wts, ill_here, spread, moves, picks, observed, estimate, inv_all)


def solution(mesh):
    placed = (
        P(None, "row", "col"),
        P(None, "row", "col"),
        P(("row", "col"), None, None, None, None),
        P("row", "col", None, None),
        P("row", "col", None, None),
        P(None, "row", "col"),
    )
    return jax.shard_map(
        functools.partial(shards, mesh.shape["row"], mesh.shape["col"]),
        mesh=mesh, in_specs=placed, out_specs=P(None, "row", "col"), check_vma=False,
    )
```

```python
import functools

import jax
import jax.numpy as jnp
import numpy as np
from jax import lax
from jax.experimental import pallas as pl
from jax.experimental.pallas import tpu as pltpu
from jax.sharding import PartitionSpec as P

MESH = pl.DeviceIdType.MESH
BF = jnp.bfloat16
F32 = jnp.float32
TAPS = 33
HALF = 16
GZ = 4
NT = (((1,), (1,)), ((), ()))


def mm(a, b):
    return jnp.dot(a, b, preferred_element_type=F32)


def mm_nt(a, b):
    return lax.dot_general(a, b, NT, preferred_element_type=F32)


def spread_table():
    w = np.zeros((128, 6 * 128), np.float32)
    for a in range(TAPS):
        plus, minus = (a - HALF) % 128, (HALF - a) % 128
        for lane in (a, TAPS + a):
            w[lane, minus] = 1.0
            w[lane, 128 + plus] = 1.0
            w[lane, 512:640] = 1.0
        w[2 * TAPS + a, 256 + plus] = 1.0
        w[2 * TAPS + a, 384 + minus] = 1.0
    w[3 * TAPS : 3 * TAPS + 3, 640:768] = 1.0
    return w.astype(BF)


def moves_table():
    eye = np.eye(128, dtype=np.float32)
    ends = np.concatenate([eye[:16], eye[112:]], 0)
    sel_r = np.zeros((GZ * 16, 128), np.float32)
    sel_l = np.zeros((GZ * 16, 128), np.float32)
    for zz in range(GZ):
        for i in range(16):
            sel_l[zz * 16 + i, zz * 32 + i] = 1.0
            sel_r[zz * 16 + i, zz * 32 + 16 + i] = 1.0
    none = np.zeros_like(sel_r)
    sel = np.block([[sel_r, none], [none, sel_l]])
    return np.concatenate([eye, ends], 0).astype(BF), sel.astype(BF)


def smoothing_table(length, n_row, rows):
    stiff = float(length * length) / 16.0
    d = np.diff(np.eye(length), axis=0)
    inv = np.linalg.inv(np.eye(length) + stiff * d.T @ d)
    rep = np.repeat(inv, rows * n_row // length, axis=1)
    return rep.reshape(length, n_row, rows).transpose(1, 0, 2).astype(np.float32)


def kernel(
    n_row, n_col, cells_hbm, ids_hbm, wts_hbm, ill_hbm, spread_hbm, moves_hbm, picks_hbm, obs_hbm, est_hbm, inv_all, out_hbm,
    cells, ids_in, wts_in, ill_in, spread, moves, picks,
    obs, est, out, wide, bank, ids, wts, ill_here, ext0, ext1, ext2, ext3, ystrip, strips, corn, cornsend, plane, ids_z, sel_send, sel_recv, ill, inv,
    base, rt0, rt1, ctc0, ctc1, cth0, cth1, ptc, pth, cur, obs_t, rfac,
    in_sem, out_sem, psend, precv, isend, irecv, bsend, brecv, lsend, lrecv, hsend, hrecv,
):
    ext = (ext0, ext1, ext2, ext3)
    rt, ctc, cth = (rt0, rt1), (ctc0, ctc1), (cth0, cth1)
    depth = obs.shape[0]
    groups = depth // GZ
    planes = n_col // 4
    row = lax.axis_index("row")
    col = lax.axis_index("col")
    zc = col // 4
    slot = lax.rem(col, 4)
    core_col = zc * 4 + slot + 1 - 2 * lax.rem(slot, 2)
    x_slot = lax.rem(slot + 2, 4)
    x_col = zc * 4 + x_slot

    def z_col(d):
        return lax.rem(zc + d + planes, planes) * 4 + slot

    up, down = lax.rem(row + n_row - 1, n_row), lax.rem(row + 1, n_row)
    left, right = lax.rem(col + n_col - 1, n_col), lax.rem(col + 1, n_col)

    barrier = pltpu.get_barrier_semaphore()
    friends = [(row, z_col(d)) for d in range(1, planes)]
    friends += [(row, core_col), (row, x_col)]
    friends += [(lax.rem(row + d, n_row), col) for d in range(1, n_row)]
    friends += [(row, left), (row, right)]
    friends += [(up, left), (up, right), (down, left), (down, right)]
    for friend in friends:
        pl.semaphore_signal(barrier, inc=1, device_id=friend, device_id_type=MESH)

    small = [
        pltpu.make_async_copy(src, dst, in_sem.at[i])
        for i, (src, dst) in enumerate([
            (cells_hbm, cells), (ids_hbm, ids_in), (wts_hbm, wts_in), (ill_hbm, ill_in),
            (moves_hbm, moves), (est_hbm, est), (spread_hbm, spread), (picks_hbm, picks),
            (obs_hbm, obs), (inv_all.at[row], inv),
        ])
    ]
    for c in small:
        c.start()

    has = {"u": row > 0, "d": row < n_row - 1, "l": col > 0, "r": col < n_col - 1}

    def there(where):
        ok = has[where[0]]
        for w in where[1:]:
            ok = jnp.logical_and(ok, has[w])
        return ok

    def zero_unless(where, refs, *at):
        @pl.when(jnp.logical_not(there(where)))
        def _():
            for ref in refs:
                part = ref.at[at]
                part[...] = jnp.zeros(part.shape, BF)

    every, low_half, high_half = slice(None), slice(0, 16), slice(16, 32)
    zero_unless("r", ext, every, slice(128, 144), slice(0, 128))
    zero_unless("l", ext, every, slice(144, 160), slice(0, 128))
    zero_unless("d", [ystrip], every, every, low_half)
    zero_unless("u", [ystrip], every, every, high_half)
    zero_unless("dr", [corn], every, every, low_half, slice(0, 128))
    zero_unless("ur", [corn], every, every, high_half, slice(0, 128))
    zero_unless("dl", [corn], every, every, low_half, slice(128, 256))
    zero_unless("ul", [corn], every, every, high_half, slice(128, 256))

    for c in small[:4]:
        c.wait()
    zones = cells.shape[0]
    lane = lax.broadcasted_iota(jnp.int32, (16, 128), 1)
    quad = lax.broadcasted_iota(jnp.int32, (16, 128), 0)
    wide[...] = jnp.zeros_like(wide)
    for i in range(zones):
        for z in range(depth):
            at = (z % GZ) * 4
            for f in range(2):
                wide[f, i, z // GZ, at : at + 4, 0:TAPS] = cells[i, z, f]
    for i in range(zones):
        for g in range(groups):
            r, c = wide[0, i, g], wide[1, i, g]
            r_hi = r.astype(BF).astype(F32)
            total_c = jnp.sum(c, -1, keepdims=True)
            s_hi = total_c.astype(BF).astype(F32)
            s_mid = (total_c - s_hi).astype(BF).astype(F32)
            packed = r_hi + pltpu.roll(r - r_hi, TAPS, 1) + pltpu.roll(c, 2 * TAPS, 1)
            packed = jnp.where(lane == 3 * TAPS, s_hi, packed)
            packed = jnp.where(lane == 3 * TAPS + 1, s_mid, packed)
            packed = jnp.where(lane == 3 * TAPS + 2, total_c - s_hi - s_mid, packed)
            bank[i, g] = packed.astype(BF)
    for g in range(groups):
        for k in range(2):
            tile_i = jnp.zeros((16, 128), F32)
            tile_w = jnp.zeros((16, 128), F32)
            for zz in range(GZ):
                here = quad // 4 == zz
                tile_i = jnp.where(here, ids_in[k, g * GZ + zz].astype(F32), tile_i)
                tile_w = jnp.where(here, wts_in[k, g * GZ + zz], tile_w)
            ids[g, k] = tile_i.astype(BF)
            wts[g, k] = tile_w
    ill_here[...] = jnp.zeros_like(ill_here)
    ill_here[:, 0 : ill_in.shape[1]] = ill_in[...]

    pl.semaphore_wait(barrier, len(friends))

    def remote(src, dst, s, r, to):
        return pltpu.make_async_remote_copy(
            src_ref=src, dst_ref=dst, send_sem=s, recv_sem=r, device_id=to, device_id_type=MESH
        )

    x_copy = remote(bank, plane.at[slot], psend.at[0], precv.at[0], (row, x_col))
    core_copy = remote(bank, plane.at[slot], psend.at[1], precv.at[1], (row, core_col))
    x_copy.start()
    core_copy.start()
    id_copies = [
        remote(ids, ids_z.at[d], isend.at[d], irecv.at[d], (row, z_col(-d))) for d in range(1, planes)
    ]
    for c in id_copies:
        c.start()
    ill_copies = [
        remote(
            ill_here, ill.at[row], lsend.at[d], lrecv.at[d], (lax.rem(row + d, n_row), col)
        )
        for d in range(1, n_row)
    ]
    for c in ill_copies:
        c.start()
    plane[slot] = bank[...]
    ids_z[0] = ids[...]
    ill[row] = ill_here[...]

    def halo_copies(p, g):
        zs = pl.ds(g * GZ, GZ)
        top, bottom = pl.ds(0, 16), pl.ds(16, 16)
        mid = pl.ds(0, 128)
        plan = [
            ("l", ext[p].at[zs, pl.ds(0, 16), mid], ext[p].at[zs, pl.ds(128, 16), mid], (row, left)),
            ("r", ext[p].at[zs, pl.ds(112, 16), mid], ext[p].at[zs, pl.ds(144, 16), mid], (row, right)),
            ("u", strips.at[p, zs, top], ystrip.at[p, zs, top], (up, col)),
            ("d", strips.at[p, zs, bottom], ystrip.at[p, zs, bottom], (down, col)),
            ("ul", cornsend.at[p, g, top], corn.at[p, g, top, pl.ds(0, 128)], (up, left)),
            ("dl", cornsend.at[p, g, bottom], corn.at[p, g, bottom, pl.ds(0, 128)], (down, left)),
            ("ur", cornsend.at[p, g, top], corn.at[p, g, top, pl.ds(128, 128)], (up, right)),
            ("dr", cornsend.at[p, g, bottom], corn.at[p, g, bottom, pl.ds(128, 128)], (down, right)),
        ]
        return [
            (where, remote(src, dst, hsend.at[p, g, i], hrecv.at[p, g, i], to))
            for i, (where, src, dst, to) in enumerate(plan)
        ]

    opposite = {"u": "d", "d": "u", "l": "r", "r": "l"}

    def halo_start(p, g):
        for where, c in halo_copies(p, g):
            @pl.when(there(where))
            def _():
                c.start()

    def halo_wait_recv(p, g):
        for where, c in halo_copies(p, g):
            @pl.when(there("".join(opposite[w] for w in where)))
            def _():
                c.wait_recv()

    def halo_wait_send(p, g):
        for where, c in halo_copies(p, g):
            @pl.when(there(where))
            def _():
                c.wait_send()

    quarter = lax.broadcasted_iota(jnp.int32, (32, 128), 1) // 32

    def pack(p, g, fields):
        for zz in range(GZ):
            ext[p][g * GZ + zz, 0:128, 0:128] = fields[zz]
        s = mm_nt(moves[128:160], jnp.concatenate(fields, 0)).astype(BF)
        for zz in range(GZ):
            strips[p, g * GZ + zz] = s[:, zz * 128 : (zz + 1) * 128]
        c = jnp.zeros((32, 128), F32)
        for zz in range(GZ):
            turned = pltpu.roll(s[:, zz * 128 : (zz + 1) * 128].astype(F32), 16 + zz * 32, 1)
            c = jnp.where(quarter == zz, turned, c)
        cornsend[p, g] = c.astype(BF)
        halo_start(p, g)

    def first_field(g):
        fields = []
        for zz in range(GZ):
            z = g * GZ + zz
            c = jnp.transpose(est[z])
            cur[z] = c
            fields.append(c.astype(BF))
        pack(0, g, fields)

    for c in small[4:6]:
        c.wait()
    pl.loop(0, groups // 2)(first_field)

    x_copy.wait_recv()
    forward = remote(plane.at[x_slot], plane.at[x_slot], psend.at[2], precv.at[2], (row, core_col))
    forward.start()
    core_copy.wait_recv()
    for c in id_copies:
        c.wait_recv()
    forward.wait_recv()

    def sel_copy(g, d):
        return remote(
            sel_send.at[g, d], sel_recv.at[g, d], bsend.at[g, d], brecv.at[g, d], (row, z_col(d))
        )

    def sel_start(g):
        for d in range(1, planes):
            sel_copy(g, d).start()

    @pl.loop(0, groups)
    def _(g):
        for d in range(planes):
            for k in range(2):
                mine = ids_z[d, g, k].astype(F32)
                picked = jnp.zeros((16, 128), F32)
                for s in range(4):
                    for i in range(4):
                        zone = (zc * 16 + s * 4 + i).astype(F32)
                        picked = jnp.where(mine == zone, plane[s, i, g].astype(F32), picked)
                sel_send[g, d, k] = picked.astype(BF)

        @pl.when(g == 0)
        def _():
            sel_start(0)

    sel_start(1)
    pl.loop(groups // 2, groups)(first_field)

    for c in small[6:]:
        c.wait()
    for c in ill_copies:
        c.wait_recv()
    coarse = ill_in.shape[1]
    fac = jnp.zeros((depth, inv.shape[1]), F32)
    for i in range(n_row):
        fac = fac + jnp.dot(
            ill[i, :, 0:coarse], inv[i * coarse : (i + 1) * coarse],
            precision=lax.Precision.HIGHEST, preferred_element_type=F32,
        )
    rfac[...] = 1.0 / fac


    def spread_taps(g):
        for d in range(1, planes):
            sel_copy(g, d).wait_recv()

        @pl.when(g + 2 < groups)
        def _():
            sel_start(g + 2)

        picked = sel_send[g, 0].astype(F32)
        for d in range(1, planes):
            picked = picked + sel_recv[g, d].astype(F32)
        b = mm(jnp.reshape(picked, (32, 128)).astype(BF), spread[...])
        r = (b[0:16], b[16:32])
        total = wts[g, 0] * r[0][:, 512:640] * r[0][:, 640:768]
        total = total + wts[g, 1] * r[1][:, 512:640] * r[1][:, 640:768]
        for shift in (1, 2):
            even = (quad // shift) % 2 == 0
            total = total + jnp.where(even, pltpu.roll(total, 16 - shift, 0), pltpu.roll(total, shift, 0))
        for k in range(2):
            for t in range(4):
                v = r[k][:, t * 128 : (t + 1) * 128]
                base[t, g, k] = (wts[g, k] * v) / total if t < 2 else v

    low = lax.broadcasted_iota(jnp.int32, (16, 128), 1) < 64
    lower = low.astype(F32).astype(BF)
    upper = 1.0 - lower

    def circulant(t, j, g, zz):
        b = jnp.broadcast_to(base[t, g, j // 4, pl.ds(zz * 4 + j % 4, 1), :], (16, 128))
        b = pltpu.roll(b, 0, 1, stride=1, stride_axis=0).astype(BF)
        return [pltpu.roll(b, 16 * i, 1) if i else b for i in range(8)]

    def build(way, g, zz):
        z = g * GZ + zz
        left_h = [0.0, 0.0]
        right_h = [0.0, 0.0]
        for j in range(8):
            js = slice(j * 128, (j + 1) * 128)
            r = circulant(way, j, g, zz)
            c = circulant(2 + way, j, g, zz)
            for i in range(1, 7):
                rt[way][z, i * 16 : i * 16 + 16, js] = r[i]
                ctc[way][z, i * 16 : i * 16 + 16, js] = c[i]
            rt[way][z, 0:16, js] = r[0] * lower
            rt[way][z, 112:128, js] = r[7] * upper
            rt[way][z, 128:144, js] = r[0] * upper
            rt[way][z, 144:160, js] = r[7] * lower
            ctc[way][z, 0:16, js] = c[0] * lower
            ctc[way][z, 112:128, js] = c[7] * upper
            at = (j % 4) * 32
            left_h[j // 4] += pltpu.roll(c[0] * upper, (at + 16 + 16) % 128, 1)
            right_h[j // 4] += pltpu.roll(c[7] * lower, at, 1) if at else c[7] * lower
        for h in range(2):
            hs = slice(h * 128, (h + 1) * 128)
            cth[way][z, 0:16, hs] = left_h[h]
            cth[way][z, 16:112, hs] = jnp.zeros((96, 128), BF)
            cth[way][z, 112:128, hs] = right_h[h]

    def out_copy(g):
        zs = pl.ds(g * GZ, GZ)
        return pltpu.make_async_copy(out.at[zs], out_hbm.at[zs], out_sem.at[g])

    def unpack(p, g):
        edges = jnp.reshape(ystrip[p, pl.ds(g * GZ, GZ)], (GZ * 32, 128))
        mid = mm_nt(moves[0:128], edges)
        corner = mm_nt(picks[...], corn[p, g]).astype(BF)
        for zz in range(GZ):
            z = g * GZ + zz
            turned = pltpu.roll(mid, 128 - zz * 32, 1) if zz else mid
            ext[p][z, 0:128, 128:160] = turned[:, 0:32].astype(BF)
            at = zz * 16
            ext[p][z, 128:144, 128:160] = corner[at : at + 16]
            at = (GZ + zz) * 16
            ext[p][z, 144:160, 128:160] = corner[at : at + 16]

    def rows_stage(p, z, zz):
        field = ext[p][z, :, 0:160]
        for jp in range(4):
            o = mm(field, rt[p % 2][z, :, jp * 256 : (jp + 1) * 256]).astype(BF)
            for h in range(2):
                j = jp * 2 + h
                ptc[zz, j * 128 : (j + 1) * 128] = o[0:128, h * 128 : (h + 1) * 128]
                pth[zz, j * 32 : (j + 1) * 32] = o[128:160, h * 128 : (h + 1) * 128]

    def cols_stage(p, z, zz):
        return mm(ctc[p % 2][z], ptc[zz]) + mm(cth[p % 2][z], pth[zz])

    for p in range(4):
        @pl.loop(0, groups)
        def _(g):
            if p == 0:
                spread_taps(g)
            if p < 2:
                @pl.loop(0, GZ)
                def _(zz):
                    build(p, g, zz)
            halo_wait_recv(p, g)
            unpack(p, g)
            fields = []
            for step in range(GZ + 1):
                if step < GZ:
                    rows_stage(p, g * GZ + step, step)
                if step == 0:
                    continue
                zz = step - 1
                z = g * GZ + zz
                f = cols_stage(p, z, zz)
                if p % 2 == 0:
                    fields.append((jnp.transpose(obs[z]) / f if p == 0 else obs_t[z] / f).astype(BF))
                    if p == 0:
                        obs_t[z] = jnp.transpose(obs[z])
                else:
                    new = cur[z] * f * rfac[pl.ds(z, 1), :]
                    if p == 3:
                        out[z] = jnp.transpose(new)
                    else:
                        cur[z] = new
                        fields.append(new.astype(BF))
            if p < 3:
                pack(p + 1, g, fields)
            else:
                out_copy(g).start()

    x_copy.wait_send()
    core_copy.wait_send()
    forward.wait_send()
    for c in id_copies + ill_copies:
        c.wait_send()
    @pl.loop(0, groups)
    def _(g):
        for d in range(1, planes):
            sel_copy(g, d).wait_send()

    for g in range(groups):
        out_copy(g).wait()
    for p in range(4):
        @pl.loop(0, groups)
        def _(g):
            halo_wait_send(p, g)


def shards(n_row, n_col, observed, estimate, psf_bank, zone_ids, mix_weights, illumination):
    depth, rows, cols = estimate.shape
    zones = psf_bank.shape[0]
    groups = depth // GZ
    planes = n_col // 4
    ids = zone_ids[0, 0].T
    wts = mix_weights[0, 0].T
    ill_here = illumination[:, :, 0]
    length = illumination.shape[1] * n_row
    spread = jnp.asarray(spread_table())
    moves, picks = map(jnp.asarray, moves_table())
    inv_all = jnp.asarray(smoothing_table(length, n_row, rows))
    hbm = pl.BlockSpec(memory_space=pl.ANY)
    dma = pltpu.SemaphoreType.DMA
    return pl.pallas_call(
        functools.partial(kernel, n_row, n_col),
        out_shape=jax.ShapeDtypeStruct(estimate.shape, F32),
        in_specs=[hbm] * 10,
        out_specs=pl.BlockSpec(memory_space=pl.ANY),
        scratch_shapes=[
            pltpu.VMEM(psf_bank.shape, F32),
            pltpu.SMEM(ids.shape, jnp.int32),
            pltpu.SMEM(wts.shape, F32),
            pltpu.VMEM(ill_here.shape, F32),
            pltpu.VMEM(spread.shape, BF),
            pltpu.VMEM(moves.shape, BF),
            pltpu.VMEM(picks.shape, BF),
            *[pltpu.VMEM((depth, rows, cols), F32)] * 3,
            pltpu.VMEM((2, zones, groups, 16, 128), F32),
            pltpu.VMEM((zones, groups, 16, 128), BF),
            pltpu.VMEM((groups, 2, 16, 128), BF),
            pltpu.VMEM((groups, 2, 16, 128), F32),
            pltpu.VMEM((depth, 128), F32),
            *[pltpu.VMEM((depth, 160, 256), BF)] * 4,
            pltpu.VMEM((4, depth, 32, 128), BF),
            pltpu.VMEM((4, depth, 32, 128), BF),
            pltpu.VMEM((4, groups, 32, 256), BF),
            pltpu.VMEM((4, groups, 32, 128), BF),
            pltpu.VMEM((4, zones, groups, 16, 128), BF),
            pltpu.VMEM((planes, groups, 2, 16, 128), BF),
            pltpu.VMEM((groups, planes, 2, 16, 128), BF),
            pltpu.VMEM((groups, planes, 2, 16, 128), BF),
            pltpu.VMEM((n_row, depth, 128), F32),
            pltpu.VMEM((length, rows), F32),
            pltpu.VMEM((4, groups, 2, 16, 128), F32),
            *[pltpu.VMEM((depth, 160, 1024), BF)] * 2,
            *[pltpu.VMEM((depth, 128, 1024), BF)] * 2,
            *[pltpu.VMEM((depth, 128, 256), BF)] * 2,
            pltpu.VMEM((GZ, 1024, 128), BF),
            pltpu.VMEM((GZ, 256, 128), BF),
            pltpu.VMEM((depth, 128, 128), F32),
            pltpu.VMEM((depth, 128, 128), F32),
            pltpu.VMEM((depth, 128), F32),
            dma((10,)), dma((groups,)),
            dma((3,)), dma((3,)),
            dma((planes,)), dma((planes,)),
            dma((groups, planes)), dma((groups, planes)),
            dma((n_row,)), dma((n_row,)),
            dma((4, groups, 8)), dma((4, groups, 8)),
        ],
        compiler_params=pltpu.CompilerParams(
            collective_id=0, has_side_effects=True, vmem_limit_bytes=60 * 2**20
        ),
        name="deconvolve",
    )(psf_bank, ids, wts, ill_here, spread, moves, picks, observed, estimate, inv_all)


def solution(mesh):
    placed = (
        P(None, "row", "col"),
        P(None, "row", "col"),
        P(("row", "col"), None, None, None, None),
        P("row", "col", None, None),
        P("row", "col", None, None),
        P(None, "row", "col"),
    )
    return jax.shard_map(
        functools.partial(shards, mesh.shape["row"], mesh.shape["col"]),
        mesh=mesh, in_specs=placed, out_specs=P(None, "row", "col"), check_vma=False,
    )
```

```python
import functools

import jax
import jax.numpy as jnp
import numpy as np
from jax import lax
from jax.experimental import pallas as pl
from jax.experimental.pallas import tpu as pltpu
from jax.sharding import PartitionSpec as P

MESH = pl.DeviceIdType.MESH
BF = jnp.bfloat16
F32 = jnp.float32
TAPS = 33
HALF = 16
GZ = 4
NT = (((1,), (1,)), ((), ()))


def mm(a, b):
    return jnp.dot(a, b, preferred_element_type=F32)


def mm_nt(a, b):
    return lax.dot_general(a, b, NT, preferred_element_type=F32)


def spread_table():
    w = np.zeros((128, 6 * 128), np.float32)
    for a in range(TAPS):
        plus, minus = (a - HALF) % 128, (HALF - a) % 128
        for lane in (a, TAPS + a):
            w[lane, minus] = 1.0
            w[lane, 128 + plus] = 1.0
            w[lane, 512:640] = 1.0
        w[2 * TAPS + a, 256 + plus] = 1.0
        w[2 * TAPS + a, 384 + minus] = 1.0
    w[3 * TAPS : 3 * TAPS + 3, 640:768] = 1.0
    return w.astype(BF)


def moves_table():
    eye = np.eye(128, dtype=np.float32)
    ends = np.concatenate([eye[:16], eye[112:]], 0)
    sel_r = np.zeros((GZ * 16, 128), np.float32)
    sel_l = np.zeros((GZ * 16, 128), np.float32)
    for zz in range(GZ):
        for i in range(16):
            sel_l[zz * 16 + i, zz * 32 + i] = 1.0
            sel_r[zz * 16 + i, zz * 32 + 16 + i] = 1.0
    none = np.zeros_like(sel_r)
    sel = np.block([[sel_r, none], [none, sel_l]])
    return np.concatenate([eye, ends], 0).astype(BF), sel.astype(BF)


def smoothing_table(length, n_row, rows):
    stiff = float(length * length) / 16.0
    d = np.diff(np.eye(length), axis=0)
    inv = np.linalg.inv(np.eye(length) + stiff * d.T @ d)
    rep = np.repeat(inv, rows * n_row // length, axis=1)
    return rep.reshape(length, n_row, rows).transpose(1, 0, 2).astype(np.float32)


def kernel(
    n_row, n_col, cells_hbm, ids_hbm, wts_hbm, ill_hbm, spread_hbm, moves_hbm, picks_hbm, obs_hbm, est_hbm, inv_all, out_hbm,
    cells, ids_in, wts_in, ill_in, spread, moves, picks,
    obs, est, out, wide, bank, ids, wts, ill_here, ext0, ext1, ext2, ext3, ystrip, strips, corn, cornsend, plane, ids_z, sel_send, sel_recv, ill, inv,
    base, rt0, rt1, ctc0, ctc1, ptc, cur, obs_t, rfac,
    in_sem, out_sem, psend, precv, isend, irecv, bsend, brecv, lsend, lrecv, hsend, hrecv,
):
    ext = (ext0, ext1, ext2, ext3)
    rt, ctc = (rt0, rt1), (ctc0, ctc1)
    depth = obs.shape[0]
    groups = depth // GZ
    planes = n_col // 4
    row = lax.axis_index("row")
    col = lax.axis_index("col")
    zc = col // 4
    slot = lax.rem(col, 4)
    core_col = zc * 4 + slot + 1 - 2 * lax.rem(slot, 2)
    x_slot = lax.rem(slot + 2, 4)
    x_col = zc * 4 + x_slot

    def z_col(d):
        return lax.rem(zc + d + planes, planes) * 4 + slot

    up, down = lax.rem(row + n_row - 1, n_row), lax.rem(row + 1, n_row)
    left, right = lax.rem(col + n_col - 1, n_col), lax.rem(col + 1, n_col)

    barrier = pltpu.get_barrier_semaphore()
    friends = [(row, z_col(d)) for d in range(1, planes)]
    friends += [(row, core_col), (row, x_col)]
    friends += [(lax.rem(row + d, n_row), col) for d in range(1, n_row)]
    friends += [(row, left), (row, right)]
    friends += [(up, left), (up, right), (down, left), (down, right)]
    for friend in friends:
        pl.semaphore_signal(barrier, inc=1, device_id=friend, device_id_type=MESH)

    small = [
        pltpu.make_async_copy(src, dst, in_sem.at[i])
        for i, (src, dst) in enumerate([
            (cells_hbm, cells), (ids_hbm, ids_in), (wts_hbm, wts_in), (ill_hbm, ill_in),
            (moves_hbm, moves), (est_hbm, est), (spread_hbm, spread), (picks_hbm, picks),
            (obs_hbm, obs), (inv_all.at[row], inv),
        ])
    ]
    for c in small:
        c.start()

    has = {"u": row > 0, "d": row < n_row - 1, "l": col > 0, "r": col < n_col - 1}

    def there(where):
        ok = has[where[0]]
        for w in where[1:]:
            ok = jnp.logical_and(ok, has[w])
        return ok

    def zero_unless(where, refs, *at):
        @pl.when(jnp.logical_not(there(where)))
        def _():
            for ref in refs:
                part = ref.at[at]
                part[...] = jnp.zeros(part.shape, BF)

    every, low_half, high_half = slice(None), slice(0, 16), slice(16, 32)
    zero_unless("r", ext, every, slice(128, 144), slice(0, 128))
    zero_unless("l", ext, every, slice(144, 160), slice(0, 128))
    zero_unless("d", [ystrip], every, every, low_half)
    zero_unless("u", [ystrip], every, every, high_half)
    zero_unless("dr", [corn], every, every, low_half, slice(0, 128))
    zero_unless("ur", [corn], every, every, high_half, slice(0, 128))
    zero_unless("dl", [corn], every, every, low_half, slice(128, 256))
    zero_unless("ul", [corn], every, every, high_half, slice(128, 256))

    for c in small[:4]:
        c.wait()
    zones = cells.shape[0]
    lane = lax.broadcasted_iota(jnp.int32, (16, 128), 1)
    quad = lax.broadcasted_iota(jnp.int32, (16, 128), 0)
    wide[...] = jnp.zeros_like(wide)
    for i in range(zones):
        for z in range(depth):
            at = (z % GZ) * 4
            for f in range(2):
                wide[f, i, z // GZ, at : at + 4, 0:TAPS] = cells[i, z, f]
    for i in range(zones):
        for g in range(groups):
            r, c = wide[0, i, g], wide[1, i, g]
            r_hi = r.astype(BF).astype(F32)
            total_c = jnp.sum(c, -1, keepdims=True)
            s_hi = total_c.astype(BF).astype(F32)
            s_mid = (total_c - s_hi).astype(BF).astype(F32)
            packed = r_hi + pltpu.roll(r - r_hi, TAPS, 1) + pltpu.roll(c, 2 * TAPS, 1)
            packed = jnp.where(lane == 3 * TAPS, s_hi, packed)
            packed = jnp.where(lane == 3 * TAPS + 1, s_mid, packed)
            packed = jnp.where(lane == 3 * TAPS + 2, total_c - s_hi - s_mid, packed)
            bank[i, g] = packed.astype(BF)
    for g in range(groups):
        for k in range(2):
            tile_i = jnp.zeros((16, 128), F32)
            tile_w = jnp.zeros((16, 128), F32)
            for zz in range(GZ):
                here = quad // 4 == zz
                tile_i = jnp.where(here, ids_in[k, g * GZ + zz].astype(F32), tile_i)
                tile_w = jnp.where(here, wts_in[k, g * GZ + zz], tile_w)
            ids[g, k] = tile_i.astype(BF)
            wts[g, k] = tile_w
    ill_here[...] = jnp.zeros_like(ill_here)
    ill_here[:, 0 : ill_in.shape[1]] = ill_in[...]

    pl.semaphore_wait(barrier, len(friends))

    def remote(src, dst, s, r, to):
        return pltpu.make_async_remote_copy(
            src_ref=src, dst_ref=dst, send_sem=s, recv_sem=r, device_id=to, device_id_type=MESH
        )

    x_copy = remote(bank, plane.at[slot], psend.at[0], precv.at[0], (row, x_col))
    core_copy = remote(bank, plane.at[slot], psend.at[1], precv.at[1], (row, core_col))
    x_copy.start()
    core_copy.start()
    id_copies = [
        remote(ids, ids_z.at[d], isend.at[d], irecv.at[d], (row, z_col(-d))) for d in range(1, planes)
    ]
    for c in id_copies:
        c.start()
    ill_copies = [
        remote(
            ill_here, ill.at[row], lsend.at[d], lrecv.at[d], (lax.rem(row + d, n_row), col)
        )
        for d in range(1, n_row)
    ]
    for c in ill_copies:
        c.start()
    plane[slot] = bank[...]
    ids_z[0] = ids[...]
    ill[row] = ill_here[...]

    def halo_copies(p, g):
        zs = pl.ds(g * GZ, GZ)
        top, bottom = pl.ds(0, 16), pl.ds(16, 16)
        mid = pl.ds(0, 128)
        plan = [
            ("l", ext[p].at[zs, pl.ds(0, 16), mid], ext[p].at[zs, pl.ds(128, 16), mid], (row, left)),
            ("r", ext[p].at[zs, pl.ds(112, 16), mid], ext[p].at[zs, pl.ds(144, 16), mid], (row, right)),
            ("u", strips.at[p, zs, top], ystrip.at[p, zs, top], (up, col)),
            ("d", strips.at[p, zs, bottom], ystrip.at[p, zs, bottom], (down, col)),
            ("ul", cornsend.at[p, g, top], corn.at[p, g, top, pl.ds(0, 128)], (up, left)),
            ("dl", cornsend.at[p, g, bottom], corn.at[p, g, bottom, pl.ds(0, 128)], (down, left)),
            ("ur", cornsend.at[p, g, top], corn.at[p, g, top, pl.ds(128, 128)], (up, right)),
            ("dr", cornsend.at[p, g, bottom], corn.at[p, g, bottom, pl.ds(128, 128)], (down, right)),
        ]
        return [
            (where, remote(src, dst, hsend.at[p, g, i], hrecv.at[p, g, i], to))
            for i, (where, src, dst, to) in enumerate(plan)
        ]

    opposite = {"u": "d", "d": "u", "l": "r", "r": "l"}

    def halo_start(p, g):
        for where, c in halo_copies(p, g):
            @pl.when(there(where))
            def _():
                c.start()

    def halo_wait_recv(p, g):
        for where, c in halo_copies(p, g):
            @pl.when(there("".join(opposite[w] for w in where)))
            def _():
                c.wait_recv()

    def halo_wait_send(p, g):
        for where, c in halo_copies(p, g):
            @pl.when(there(where))
            def _():
                c.wait_send()

    quarter = lax.broadcasted_iota(jnp.int32, (32, 128), 1) // 32

    def pack(p, g, fields):
        for zz in range(GZ):
            ext[p][g * GZ + zz, 0:128, 0:128] = fields[zz]
        s = mm_nt(moves[128:160], jnp.concatenate(fields, 0)).astype(BF)
        for zz in range(GZ):
            strips[p, g * GZ + zz] = s[:, zz * 128 : (zz + 1) * 128]
        c = jnp.zeros((32, 128), F32)
        for zz in range(GZ):
            turned = pltpu.roll(s[:, zz * 128 : (zz + 1) * 128].astype(F32), 16 + zz * 32, 1)
            c = jnp.where(quarter == zz, turned, c)
        cornsend[p, g] = c.astype(BF)
        halo_start(p, g)

    def first_field(g):
        fields = []
        for zz in range(GZ):
            z = g * GZ + zz
            c = jnp.transpose(est[z])
            cur[z] = c
            fields.append(c.astype(BF))
        pack(0, g, fields)

    for c in small[4:6]:
        c.wait()
    pl.loop(0, groups // 2)(first_field)

    x_copy.wait_recv()
    forward = remote(plane.at[x_slot], plane.at[x_slot], psend.at[2], precv.at[2], (row, core_col))
    forward.start()
    core_copy.wait_recv()
    for c in id_copies:
        c.wait_recv()
    forward.wait_recv()

    def sel_copy(g, d):
        return remote(
            sel_send.at[g, d], sel_recv.at[g, d], bsend.at[g, d], brecv.at[g, d], (row, z_col(d))
        )

    def sel_start(g):
        for d in range(1, planes):
            sel_copy(g, d).start()

    @pl.loop(0, groups)
    def _(g):
        for d in range(planes):
            for k in range(2):
                mine = ids_z[d, g, k].astype(F32)
                picked = jnp.zeros((16, 128), F32)
                for s in range(4):
                    for i in range(4):
                        zone = (zc * 16 + s * 4 + i).astype(F32)
                        picked = jnp.where(mine == zone, plane[s, i, g].astype(F32), picked)
                sel_send[g, d, k] = picked.astype(BF)

        @pl.when(g == 0)
        def _():
            sel_start(0)

    sel_start(1)
    pl.loop(groups // 2, groups)(first_field)

    for c in small[6:]:
        c.wait()
    for c in ill_copies:
        c.wait_recv()
    coarse = ill_in.shape[1]
    fac = jnp.zeros((depth, inv.shape[1]), F32)
    for i in range(n_row):
        fac = fac + jnp.dot(
            ill[i, :, 0:coarse], inv[i * coarse : (i + 1) * coarse],
            precision=lax.Precision.HIGHEST, preferred_element_type=F32,
        )
    rfac[...] = 1.0 / fac


    def spread_taps(g):
        for d in range(1, planes):
            sel_copy(g, d).wait_recv()

        @pl.when(g + 2 < groups)
        def _():
            sel_start(g + 2)

        picked = sel_send[g, 0].astype(F32)
        for d in range(1, planes):
            picked = picked + sel_recv[g, d].astype(F32)
        b = mm(jnp.reshape(picked, (32, 128)).astype(BF), spread[...])
        r = (b[0:16], b[16:32])
        total = wts[g, 0] * r[0][:, 512:640] * r[0][:, 640:768]
        total = total + wts[g, 1] * r[1][:, 512:640] * r[1][:, 640:768]
        for shift in (1, 2):
            even = (quad // shift) % 2 == 0
            total = total + jnp.where(even, pltpu.roll(total, 16 - shift, 0), pltpu.roll(total, shift, 0))
        for k in range(2):
            for t in range(4):
                v = r[k][:, t * 128 : (t + 1) * 128]
                base[t, g, k] = (wts[g, k] * v) / total if t < 2 else v

    low = lax.broadcasted_iota(jnp.int32, (16, 128), 1) < 64
    lower = low.astype(F32).astype(BF)
    upper = 1.0 - lower

    def circulant(t, j, g, zz):
        b = jnp.broadcast_to(base[t, g, j // 4, pl.ds(zz * 4 + j % 4, 1), :], (16, 128))
        b = pltpu.roll(b, 0, 1, stride=1, stride_axis=0).astype(BF)
        return [pltpu.roll(b, 16 * i, 1) if i else b for i in range(8)]

    def build(way, g, zz):
        z = g * GZ + zz
        left_h = [0.0, 0.0]
        right_h = [0.0, 0.0]
        for j in range(8):
            js = slice(j * 128, (j + 1) * 128)
            r = circulant(way, j, g, zz)
            c = circulant(2 + way, j, g, zz)
            for i in range(1, 7):
                rt[way][z, i * 16 : i * 16 + 16, js] = r[i]
                ctc[way][z, i * 16 : i * 16 + 16, js] = c[i]
            rt[way][z, 0:16, js] = r[0] * lower
            rt[way][z, 112:128, js] = r[7] * upper
            rt[way][z, 128:144, js] = r[0] * upper
            rt[way][z, 144:160, js] = r[7] * lower
            ctc[way][z, 0:16, js] = c[0] * lower
            ctc[way][z, 112:128, js] = c[7] * upper
            at = (j % 4) * 32
            left_h[j // 4] += pltpu.roll(c[0] * upper, (at + 16 + 16) % 128, 1)
            right_h[j // 4] += pltpu.roll(c[7] * lower, at, 1) if at else c[7] * lower
        for h in range(2):
            hs = slice(1024 + h * 128, 1152 + h * 128)
            ctc[way][z, 0:16, hs] = left_h[h]
            ctc[way][z, 16:112, hs] = jnp.zeros((96, 128), BF)
            ctc[way][z, 112:128, hs] = right_h[h]

    def out_copy(g):
        zs = pl.ds(g * GZ, GZ)
        return pltpu.make_async_copy(out.at[zs], out_hbm.at[zs], out_sem.at[g])

    def unpack(p, g):
        edges = jnp.reshape(ystrip[p, pl.ds(g * GZ, GZ)], (GZ * 32, 128))
        mid = mm_nt(moves[0:128], edges)
        corner = mm_nt(picks[...], corn[p, g]).astype(BF)
        for zz in range(GZ):
            z = g * GZ + zz
            turned = pltpu.roll(mid, 128 - zz * 32, 1) if zz else mid
            ext[p][z, 0:128, 128:160] = turned[:, 0:32].astype(BF)
            at = zz * 16
            ext[p][z, 128:144, 128:160] = corner[at : at + 16]
            at = (GZ + zz) * 16
            ext[p][z, 144:160, 128:160] = corner[at : at + 16]

    def rows_stage(p, z, zz):
        field = ext[p][z, :, 0:160]
        for jp in range(4):
            o = mm(field, rt[p % 2][z, :, jp * 256 : (jp + 1) * 256]).astype(BF)
            for h in range(2):
                j = jp * 2 + h
                ptc[zz, j * 128 : (j + 1) * 128] = o[0:128, h * 128 : (h + 1) * 128]
                ptc[zz, 1024 + j * 32 : 1056 + j * 32] = o[128:160, h * 128 : (h + 1) * 128]

    def cols_stage(p, z, zz):
        return mm(ctc[p % 2][z], ptc[zz])

    for p in range(4):
        @pl.loop(0, groups)
        def _(g):
            if p == 0:
                spread_taps(g)
            if p < 2:
                @pl.loop(0, GZ)
                def _(zz):
                    build(p, g, zz)
            halo_wait_recv(p, g)
            unpack(p, g)
            fields = []
            for step in range(GZ + 1):
                if step < GZ:
                    rows_stage(p, g * GZ + step, step)
                if step == 0:
                    continue
                zz = step - 1
                z = g * GZ + zz
                f = cols_stage(p, z, zz)
                if p % 2 == 0:
                    fields.append((jnp.transpose(obs[z]) / f if p == 0 else obs_t[z] / f).astype(BF))
                    if p == 0:
                        obs_t[z] = jnp.transpose(obs[z])
                else:
                    new = cur[z] * f * rfac[pl.ds(z, 1), :]
                    if p == 3:
                        out[z] = jnp.transpose(new)
                    else:
                        cur[z] = new
                        fields.append(new.astype(BF))
            if p < 3:
                pack(p + 1, g, fields)
            else:
                out_copy(g).start()

    x_copy.wait_send()
    core_copy.wait_send()
    forward.wait_send()
    for c in id_copies + ill_copies:
        c.wait_send()
    @pl.loop(0, groups)
    def _(g):
        for d in range(1, planes):
            sel_copy(g, d).wait_send()

    for g in range(groups):
        out_copy(g).wait()
    for p in range(4):
        @pl.loop(0, groups)
        def _(g):
            halo_wait_send(p, g)


def shards(n_row, n_col, observed, estimate, psf_bank, zone_ids, mix_weights, illumination):
    depth, rows, cols = estimate.shape
    zones = psf_bank.shape[0]
    groups = depth // GZ
    planes = n_col // 4
    ids = zone_ids[0, 0].T
    wts = mix_weights[0, 0].T
    ill_here = illumination[:, :, 0]
    length = illumination.shape[1] * n_row
    spread = jnp.asarray(spread_table())
    moves, picks = map(jnp.asarray, moves_table())
    inv_all = jnp.asarray(smoothing_table(length, n_row, rows))
    hbm = pl.BlockSpec(memory_space=pl.ANY)
    dma = pltpu.SemaphoreType.DMA
    return pl.pallas_call(
        functools.partial(kernel, n_row, n_col),
        out_shape=jax.ShapeDtypeStruct(estimate.shape, F32),
        in_specs=[hbm] * 10,
        out_specs=pl.BlockSpec(memory_space=pl.ANY),
        scratch_shapes=[
            pltpu.VMEM(psf_bank.shape, F32),
            pltpu.SMEM(ids.shape, jnp.int32),
            pltpu.SMEM(wts.shape, F32),
            pltpu.VMEM(ill_here.shape, F32),
            pltpu.VMEM(spread.shape, BF),
            pltpu.VMEM(moves.shape, BF),
            pltpu.VMEM(picks.shape, BF),
            *[pltpu.VMEM((depth, rows, cols), F32)] * 3,
            pltpu.VMEM((2, zones, groups, 16, 128), F32),
            pltpu.VMEM((zones, groups, 16, 128), BF),
            pltpu.VMEM((groups, 2, 16, 128), BF),
            pltpu.VMEM((groups, 2, 16, 128), F32),
            pltpu.VMEM((depth, 128), F32),
            *[pltpu.VMEM((depth, 160, 256), BF)] * 4,
            pltpu.VMEM((4, depth, 32, 128), BF),
            pltpu.VMEM((4, depth, 32, 128), BF),
            pltpu.VMEM((4, groups, 32, 256), BF),
            pltpu.VMEM((4, groups, 32, 128), BF),
            pltpu.VMEM((4, zones, groups, 16, 128), BF),
            pltpu.VMEM((planes, groups, 2, 16, 128), BF),
            pltpu.VMEM((groups, planes, 2, 16, 128), BF),
            pltpu.VMEM((groups, planes, 2, 16, 128), BF),
            pltpu.VMEM((n_row, depth, 128), F32),
            pltpu.VMEM((length, rows), F32),
            pltpu.VMEM((4, groups, 2, 16, 128), F32),
            *[pltpu.VMEM((depth, 160, 1024), BF)] * 2,
            *[pltpu.VMEM((depth, 128, 1280), BF)] * 2,
            pltpu.VMEM((GZ, 1280, 128), BF),
            pltpu.VMEM((depth, 128, 128), F32),
            pltpu.VMEM((depth, 128, 128), F32),
            pltpu.VMEM((depth, 128), F32),
            dma((10,)), dma((groups,)),
            dma((3,)), dma((3,)),
            dma((planes,)), dma((planes,)),
            dma((groups, planes)), dma((groups, planes)),
            dma((n_row,)), dma((n_row,)),
            dma((4, groups, 8)), dma((4, groups, 8)),
        ],
        compiler_params=pltpu.CompilerParams(
            collective_id=0, has_side_effects=True, vmem_limit_bytes=44 * 2**20
        ),
        name="deconvolve",
    )(*[pltpu.with_memory_space_constraint(v, pltpu.HBM) for v in (psf_bank, ids, wts, ill_here, spread, moves, picks, observed, estimate, inv_all)])


def solution(mesh):
    placed = (
        P(None, "row", "col"),
        P(None, "row", "col"),
        P(("row", "col"), None, None, None, None),
        P("row", "col", None, None),
        P("row", "col", None, None),
        P(None, "row", "col"),
    )
    return jax.shard_map(
        functools.partial(shards, mesh.shape["row"], mesh.shape["col"]),
        mesh=mesh, in_specs=placed, out_specs=P(None, "row", "col"), check_vma=False,
    )
```

```python
import functools

import jax
import jax.numpy as jnp
import numpy as np
from jax import lax
from jax.experimental import pallas as pl
from jax.experimental.pallas import tpu as pltpu
from jax.sharding import PartitionSpec as P

MESH = pl.DeviceIdType.MESH
BF = jnp.bfloat16
F32 = jnp.float32
TAPS = 33
HALF = 16
GZ = 4
NT = (((1,), (1,)), ((), ()))


def mm(a, b):
    return jnp.dot(a, b, preferred_element_type=F32)


def mm_nt(a, b):
    return lax.dot_general(a, b, NT, preferred_element_type=F32)


def spread_table():
    w = np.zeros((128, 6 * 128), np.float32)
    for a in range(TAPS):
        plus, minus = (a - HALF) % 128, (HALF - a) % 128
        for lane in (a, TAPS + a):
            w[lane, minus] = 1.0
            w[lane, 128 + plus] = 1.0
            w[lane, 512:640] = 1.0
        w[2 * TAPS + a, 256 + plus] = 1.0
        w[2 * TAPS + a, 384 + minus] = 1.0
    w[3 * TAPS : 3 * TAPS + 3, 640:768] = 1.0
    return w.astype(BF)


def moves_table():
    eye = np.eye(128, dtype=np.float32)
    ends = np.concatenate([eye[:16], eye[112:]], 0)
    sel_r = np.zeros((GZ * 16, 128), np.float32)
    sel_l = np.zeros((GZ * 16, 128), np.float32)
    for zz in range(GZ):
        for i in range(16):
            sel_l[zz * 16 + i, zz * 32 + i] = 1.0
            sel_r[zz * 16 + i, zz * 32 + 16 + i] = 1.0
    none = np.zeros_like(sel_r)
    sel = np.block([[sel_r, none], [none, sel_l]])
    return np.concatenate([eye, ends], 0).astype(BF), sel.astype(BF)


def smoothing_table(length, n_row, rows):
    stiff = float(length * length) / 16.0
    d = np.diff(np.eye(length), axis=0)
    inv = np.linalg.inv(np.eye(length) + stiff * d.T @ d)
    rep = np.repeat(inv, rows * n_row // length, axis=1)
    return rep.reshape(length, n_row, rows).transpose(1, 0, 2).astype(np.float32)


def kernel(
    n_row, n_col, cells_hbm, ids_hbm, wts_hbm, ill_hbm, spread_hbm, moves_hbm, picks_hbm, obs_hbm, est_hbm, inv_all, out_hbm,
    cells, ids_in, wts_in, ill_in, spread, moves, picks,
    obs, est, out, wide, bank, ids, wts, ill_here, ext0, ext1, ext2, ext3, ystrip, strips, corn, cornsend, plane, ids_z, sel_send, sel_recv, ill, inv,
    base, rt0, rt1, ctc0, ctc1, ptc, cur, obs_t, rfac,
    in_sem, out_sem, psend, precv, isend, irecv, bsend, brecv, lsend, lrecv, hsend, hrecv,
):
    ext = (ext0, ext1, ext2, ext3)
    rt, ctc = (rt0, rt1), (ctc0, ctc1)
    depth = obs.shape[0]
    groups = depth // GZ
    planes = n_col // 4
    row = lax.axis_index("row")
    col = lax.axis_index("col")
    zc = col // 4
    slot = lax.rem(col, 4)
    core_col = zc * 4 + slot + 1 - 2 * lax.rem(slot, 2)
    x_col = zc * 4 + lax.rem(slot + 2, 4)

    def z_col(d):
        return lax.rem(zc + d + planes, planes) * 4 + slot

    up, down = lax.rem(row + n_row - 1, n_row), lax.rem(row + 1, n_row)
    left, right = lax.rem(col + n_col - 1, n_col), lax.rem(col + 1, n_col)

    barrier = pltpu.get_barrier_semaphore()
    friends = [(row, z_col(d)) for d in range(1, planes)]
    friends += [(row, core_col), (row, x_col), (row, zc * 4 + 3 - slot)]
    friends += [(lax.rem(row + d, n_row), col) for d in range(1, n_row)]
    friends += [(row, left), (row, right)]
    friends += [(up, left), (up, right), (down, left), (down, right)]
    for friend in friends:
        pl.semaphore_signal(barrier, inc=1, device_id=friend, device_id_type=MESH)

    small = [
        pltpu.make_async_copy(src, dst, in_sem.at[i])
        for i, (src, dst) in enumerate([
            (cells_hbm, cells), (ids_hbm, ids_in), (wts_hbm, wts_in), (ill_hbm, ill_in),
            (moves_hbm, moves), (est_hbm, est), (spread_hbm, spread), (picks_hbm, picks),
            (obs_hbm, obs), (inv_all.at[row], inv),
        ])
    ]
    for c in small:
        c.start()

    has = {"u": row > 0, "d": row < n_row - 1, "l": col > 0, "r": col < n_col - 1}

    def there(where):
        ok = has[where[0]]
        for w in where[1:]:
            ok = jnp.logical_and(ok, has[w])
        return ok

    def zero_unless(where, refs, *at):
        @pl.when(jnp.logical_not(there(where)))
        def _():
            for ref in refs:
                part = ref.at[at]
                part[...] = jnp.zeros(part.shape, BF)

    every, low_half, high_half = slice(None), slice(0, 16), slice(16, 32)
    zero_unless("r", ext, every, slice(128, 144), slice(0, 128))
    zero_unless("l", ext, every, slice(144, 160), slice(0, 128))
    zero_unless("d", [ystrip], every, every, low_half)
    zero_unless("u", [ystrip], every, every, high_half)
    zero_unless("dr", [corn], every, every, low_half, slice(0, 128))
    zero_unless("ur", [corn], every, every, high_half, slice(0, 128))
    zero_unless("dl", [corn], every, every, low_half, slice(128, 256))
    zero_unless("ul", [corn], every, every, high_half, slice(128, 256))

    for c in small[:4]:
        c.wait()
    zones = cells.shape[0]
    lane = lax.broadcasted_iota(jnp.int32, (16, 128), 1)
    quad = lax.broadcasted_iota(jnp.int32, (16, 128), 0)
    wide[...] = jnp.zeros_like(wide)
    for i in range(zones):
        for z in range(depth):
            at = (z % GZ) * 4
            for f in range(2):
                wide[f, i, z // GZ, at : at + 4, 0:TAPS] = cells[i, z, f]
    for i in range(zones):
        for g in range(groups):
            r, c = wide[0, i, g], wide[1, i, g]
            r_hi = r.astype(BF).astype(F32)
            total_c = jnp.sum(c, -1, keepdims=True)
            s_hi = total_c.astype(BF).astype(F32)
            s_mid = (total_c - s_hi).astype(BF).astype(F32)
            packed = r_hi + pltpu.roll(r - r_hi, TAPS, 1) + pltpu.roll(c, 2 * TAPS, 1)
            packed = jnp.where(lane == 3 * TAPS, s_hi, packed)
            packed = jnp.where(lane == 3 * TAPS + 1, s_mid, packed)
            packed = jnp.where(lane == 3 * TAPS + 2, total_c - s_hi - s_mid, packed)
            bank[g, i] = packed.astype(BF)
    tile_i = jnp.zeros((16, 128), F32)
    for g in range(groups):
        for k in range(2):
            lanes_here = lane // 16 == g * 2 + k
            tile_w = jnp.zeros((16, 128), F32)
            for zz in range(GZ):
                here = quad // 4 == zz
                both = jnp.logical_and(here, lanes_here)
                tile_i = jnp.where(both, ids_in[k, g * GZ + zz].astype(F32), tile_i)
                tile_w = jnp.where(here, wts_in[k, g * GZ + zz], tile_w)
            wts[g, k] = tile_w
    ids[...] = tile_i.astype(BF)
    ill_here[...] = jnp.zeros_like(ill_here)
    ill_here[:, 0 : ill_in.shape[1]] = ill_in[...]

    pl.semaphore_wait(barrier, len(friends))

    def remote(src, dst, s, r, to):
        return pltpu.make_async_remote_copy(
            src_ref=src, dst_ref=dst, send_sem=s, recv_sem=r, device_id=to, device_id_type=MESH
        )

    far_col = zc * 4 + 3 - slot

    def plane_copies(g):
        return [
            remote(bank.at[g], plane.at[g, slot], psend.at[g, i], precv.at[g, i], (row, to))
            for i, to in enumerate((x_col, far_col, core_col))
        ]

    def plane_start(g):
        for c in plane_copies(g):
            c.start()

    plane_start(0)
    id_copies = [
        remote(ids, ids_z.at[d], isend.at[d], irecv.at[d], (row, z_col(-d))) for d in range(1, planes)
    ]
    for c in id_copies:
        c.start()
    ill_copies = [
        remote(
            ill_here, ill.at[row], lsend.at[d], lrecv.at[d], (lax.rem(row + d, n_row), col)
        )
        for d in range(1, n_row)
    ]
    for g in range(groups):
        plane[g, slot] = bank[g]
    ids_z[0] = ids[...]
    ill[row] = ill_here[...]

    def halo_copies(p, g):
        zs = pl.ds(g * GZ, GZ)
        top, bottom = pl.ds(0, 16), pl.ds(16, 16)
        mid = pl.ds(0, 128)
        plan = [
            ("l", ext[p].at[zs, pl.ds(0, 16), mid], ext[p].at[zs, pl.ds(128, 16), mid], (row, left)),
            ("r", ext[p].at[zs, pl.ds(112, 16), mid], ext[p].at[zs, pl.ds(144, 16), mid], (row, right)),
            ("u", strips.at[p, zs, top], ystrip.at[p, zs, top], (up, col)),
            ("d", strips.at[p, zs, bottom], ystrip.at[p, zs, bottom], (down, col)),
            ("ul", cornsend.at[p, g, top], corn.at[p, g, top, pl.ds(0, 128)], (up, left)),
            ("dl", cornsend.at[p, g, bottom], corn.at[p, g, bottom, pl.ds(0, 128)], (down, left)),
            ("ur", cornsend.at[p, g, top], corn.at[p, g, top, pl.ds(128, 128)], (up, right)),
            ("dr", cornsend.at[p, g, bottom], corn.at[p, g, bottom, pl.ds(128, 128)], (down, right)),
        ]
        return [
            (where, remote(src, dst, hsend.at[p, g, i], hrecv.at[p, g, i], to))
            for i, (where, src, dst, to) in enumerate(plan)
        ]

    opposite = {"u": "d", "d": "u", "l": "r", "r": "l"}

    def halo_start(p, g):
        for where, c in halo_copies(p, g):
            @pl.when(there(where))
            def _():
                c.start()

    def halo_wait_recv(p, g):
        for where, c in halo_copies(p, g):
            @pl.when(there("".join(opposite[w] for w in where)))
            def _():
                c.wait_recv()

    def halo_wait_send(p, g):
        for where, c in halo_copies(p, g):
            @pl.when(there(where))
            def _():
                c.wait_send()

    quarter = lax.broadcasted_iota(jnp.int32, (32, 128), 1) // 32

    def pack(p, g, fields):
        for zz in range(GZ):
            ext[p][g * GZ + zz, 0:128, 0:128] = fields[zz]
        s = mm_nt(moves[128:160], jnp.concatenate(fields, 0)).astype(BF)
        for zz in range(GZ):
            strips[p, g * GZ + zz] = s[:, zz * 128 : (zz + 1) * 128]
        c = jnp.zeros((32, 128), F32)
        for zz in range(GZ):
            turned = pltpu.roll(s[:, zz * 128 : (zz + 1) * 128].astype(F32), 16 + zz * 32, 1)
            c = jnp.where(quarter == zz, turned, c)
        cornsend[p, g] = c.astype(BF)
        halo_start(p, g)

    def first_field(g):
        fields = []
        for zz in range(GZ):
            z = g * GZ + zz
            c = jnp.transpose(est[z])
            cur[z] = c
            fields.append(c.astype(BF))
        pack(0, g, fields)

    for c in small[4:6]:
        c.wait()
    for g in range(groups):
        if g:
            plane_start(g)
        first_field(g)
    for c in ill_copies:
        c.start()

    for c in id_copies:
        c.wait_recv()

    def sel_copy(g, d):
        return remote(
            sel_send.at[g, d], sel_recv.at[g, d], bsend.at[g, d], brecv.at[g, d], (row, z_col(d))
        )

    def select(g):
        for c in plane_copies(g):
            c.wait_recv()
        for d in range(planes):
            for k in range(2):
                one = jnp.where(lane == (g * 2 + k) * 16, ids_z[d].astype(F32), 0.0)
                mine = jnp.broadcast_to(jnp.sum(one, -1, keepdims=True), (16, 128))
                picked = jnp.zeros((16, 128), F32)
                for s in range(4):
                    for i in range(4):
                        zone = (zc * 16 + s * 4 + i).astype(F32)
                        picked = jnp.where(mine == zone, plane[g, s, i].astype(F32), picked)
                sel_send[g, d, k] = picked.astype(BF)
        for d in range(1, planes):
            sel_copy(g, d).start()

    pl.loop(0, 2)(select)

    for c in small[6:]:
        c.wait()

    def smooth():
        for c in ill_copies:
            c.wait_recv()
        coarse = ill_in.shape[1]
        fac = jnp.zeros((depth, inv.shape[1]), F32)
        for i in range(n_row):
            fac = fac + jnp.dot(
                ill[i, :, 0:coarse], inv[i * coarse : (i + 1) * coarse],
                precision=lax.Precision.HIGHEST, preferred_element_type=F32,
            )
        rfac[...] = 1.0 / fac

    def spread_taps(g):
        for d in range(1, planes):
            sel_copy(g, d).wait_recv()

        @pl.when(g + 2 < groups)
        def _():
            select(g + 2)

        picked = sel_send[g, 0].astype(F32)
        for d in range(1, planes):
            picked = picked + sel_recv[g, d].astype(F32)
        b = mm(jnp.reshape(picked, (32, 128)).astype(BF), spread[...])
        r = (b[0:16], b[16:32])
        total = wts[g, 0] * r[0][:, 512:640] * r[0][:, 640:768]
        total = total + wts[g, 1] * r[1][:, 512:640] * r[1][:, 640:768]
        for shift in (1, 2):
            even = (quad // shift) % 2 == 0
            total = total + jnp.where(even, pltpu.roll(total, 16 - shift, 0), pltpu.roll(total, shift, 0))
        for k in range(2):
            for t in range(4):
                v = r[k][:, t * 128 : (t + 1) * 128]
                base[t, g, k] = (wts[g, k] * v) / total if t < 2 else v

    low = lax.broadcasted_iota(jnp.int32, (16, 128), 1) < 64
    lower = low.astype(F32).astype(BF)
    upper = 1.0 - lower

    def circulant(t, j, g, zz):
        b = jnp.broadcast_to(base[t, g, j // 4, pl.ds(zz * 4 + j % 4, 1), :], (16, 128))
        b = pltpu.roll(b, 0, 1, stride=1, stride_axis=0).astype(BF)
        return [pltpu.roll(b, 16 * i, 1) if i else b for i in range(8)]

    def build(way, g, zz):
        z = g * GZ + zz
        left_h = [0.0, 0.0]
        right_h = [0.0, 0.0]
        for j in range(8):
            js = slice(j * 128, (j + 1) * 128)
            r = circulant(way, j, g, zz)
            c = circulant(2 + way, j, g, zz)
            for i in range(1, 7):
                rt[way][z, i * 16 : i * 16 + 16, js] = r[i]
                ctc[way][z, i * 16 : i * 16 + 16, js] = c[i]
            rt[way][z, 0:16, js] = r[0] * lower
            rt[way][z, 112:128, js] = r[7] * upper
            rt[way][z, 128:144, js] = r[0] * upper
            rt[way][z, 144:160, js] = r[7] * lower
            ctc[way][z, 0:16, js] = c[0] * lower
            ctc[way][z, 112:128, js] = c[7] * upper
            at = (j % 4) * 32
            left_h[j // 4] += pltpu.roll(c[0] * upper, (at + 16 + 16) % 128, 1)
            right_h[j // 4] += pltpu.roll(c[7] * lower, at, 1) if at else c[7] * lower
        for h in range(2):
            hs = slice(1024 + h * 128, 1152 + h * 128)
            ctc[way][z, 0:16, hs] = left_h[h]
            ctc[way][z, 16:112, hs] = jnp.zeros((96, 128), BF)
            ctc[way][z, 112:128, hs] = right_h[h]

    def out_copy(g):
        zs = pl.ds(g * GZ, GZ)
        return pltpu.make_async_copy(out.at[zs], out_hbm.at[zs], out_sem.at[g])

    def unpack(p, g):
        edges = jnp.reshape(ystrip[p, pl.ds(g * GZ, GZ)], (GZ * 32, 128))
        mid = mm_nt(moves[0:128], edges)
        corner = mm_nt(picks[...], corn[p, g]).astype(BF)
        for zz in range(GZ):
            z = g * GZ + zz
            turned = pltpu.roll(mid, 128 - zz * 32, 1) if zz else mid
            ext[p][z, 0:128, 128:160] = turned[:, 0:32].astype(BF)
            at = zz * 16
            ext[p][z, 128:144, 128:160] = corner[at : at + 16]
            at = (GZ + zz) * 16
            ext[p][z, 144:160, 128:160] = corner[at : at + 16]

    def rows_stage(p, z, zz):
        field = ext[p][z, :, 0:160]
        for jp in range(4):
            o = mm(field, rt[p % 2][z, :, jp * 256 : (jp + 1) * 256]).astype(BF)
            for h in range(2):
                j = jp * 2 + h
                ptc[zz, j * 128 : (j + 1) * 128] = o[0:128, h * 128 : (h + 1) * 128]
                ptc[zz, 1024 + j * 32 : 1056 + j * 32] = o[128:160, h * 128 : (h + 1) * 128]

    def cols_stage(p, z, zz):
        return mm(ctc[p % 2][z], ptc[zz])

    for p in range(4):
        if p == 1:
            smooth()

        @pl.loop(0, groups)
        def _(g):
            if p == 0:
                spread_taps(g)
            if p < 2:
                @pl.loop(0, GZ)
                def _(zz):
                    build(p, g, zz)
            halo_wait_recv(p, g)
            unpack(p, g)
            fields = []
            for step in range(GZ + 1):
                if step < GZ:
                    rows_stage(p, g * GZ + step, step)
                if step == 0:
                    continue
                zz = step - 1
                z = g * GZ + zz
                f = cols_stage(p, z, zz)
                if p % 2 == 0:
                    fields.append((jnp.transpose(obs[z]) / f if p == 0 else obs_t[z] / f).astype(BF))
                    if p == 0:
                        obs_t[z] = jnp.transpose(obs[z])
                else:
                    new = cur[z] * f * rfac[pl.ds(z, 1), :]
                    if p == 3:
                        out[z] = jnp.transpose(new)
                    else:
                        cur[z] = new
                        fields.append(new.astype(BF))
            if p < 3:
                pack(p + 1, g, fields)
            else:
                out_copy(g).start()

    for g in range(groups):
        for c in plane_copies(g):
            c.wait_send()
    for c in id_copies + ill_copies:
        c.wait_send()
    @pl.loop(0, groups)
    def _(g):
        for d in range(1, planes):
            sel_copy(g, d).wait_send()

    for g in range(groups):
        out_copy(g).wait()
    for p in range(4):
        @pl.loop(0, groups)
        def _(g):
            halo_wait_send(p, g)


def shards(n_row, n_col, observed, estimate, psf_bank, zone_ids, mix_weights, illumination):
    depth, rows, cols = estimate.shape
    zones = psf_bank.shape[0]
    groups = depth // GZ
    planes = n_col // 4
    ids = zone_ids[0, 0].T
    wts = mix_weights[0, 0].T
    ill_here = illumination[:, :, 0]
    length = illumination.shape[1] * n_row
    spread = jnp.asarray(spread_table())
    moves, picks = map(jnp.asarray, moves_table())
    inv_all = jnp.asarray(smoothing_table(length, n_row, rows))
    hbm = pl.BlockSpec(memory_space=pl.ANY)
    dma = pltpu.SemaphoreType.DMA
    return pl.pallas_call(
        functools.partial(kernel, n_row, n_col),
        out_shape=jax.ShapeDtypeStruct(estimate.shape, F32),
        in_specs=[hbm] * 10,
        out_specs=pl.BlockSpec(memory_space=pl.ANY),
        scratch_shapes=[
            pltpu.VMEM(psf_bank.shape, F32),
            pltpu.SMEM(ids.shape, jnp.int32),
            pltpu.SMEM(wts.shape, F32),
            pltpu.VMEM(ill_here.shape, F32),
            pltpu.VMEM(spread.shape, BF),
            pltpu.VMEM(moves.shape, BF),
            pltpu.VMEM(picks.shape, BF),
            *[pltpu.VMEM((depth, rows, cols), F32)] * 3,
            pltpu.VMEM((2, zones, groups, 16, 128), F32),
            pltpu.VMEM((groups, zones, 16, 128), BF),
            pltpu.VMEM((16, 128), BF),
            pltpu.VMEM((groups, 2, 16, 128), F32),
            pltpu.VMEM((depth, 128), F32),
            *[pltpu.VMEM((depth, 160, 256), BF)] * 4,
            pltpu.VMEM((4, depth, 32, 128), BF),
            pltpu.VMEM((4, depth, 32, 128), BF),
            pltpu.VMEM((4, groups, 32, 256), BF),
            pltpu.VMEM((4, groups, 32, 128), BF),
            pltpu.VMEM((groups, 4, zones, 16, 128), BF),
            pltpu.VMEM((planes, 16, 128), BF),
            pltpu.VMEM((groups, planes, 2, 16, 128), BF),
            pltpu.VMEM((groups, planes, 2, 16, 128), BF),
            pltpu.VMEM((n_row, depth, 128), F32),
            pltpu.VMEM((length, rows), F32),
            pltpu.VMEM((4, groups, 2, 16, 128), F32),
            *[pltpu.VMEM((depth, 160, 1024), BF)] * 2,
            *[pltpu.VMEM((depth, 128, 1280), BF)] * 2,
            pltpu.VMEM((GZ, 1280, 128), BF),
            pltpu.VMEM((depth, 128, 128), F32),
            pltpu.VMEM((depth, 128, 128), F32),
            pltpu.VMEM((depth, 128), F32),
            dma((10,)), dma((groups,)),
            dma((groups, 3)), dma((groups, 3)),
            dma((planes,)), dma((planes,)),
            dma((groups, planes)), dma((groups, planes)),
            dma((n_row,)), dma((n_row,)),
            dma((4, groups, 8)), dma((4, groups, 8)),
        ],
        compiler_params=pltpu.CompilerParams(
            collective_id=0, has_side_effects=True, vmem_limit_bytes=44 * 2**20
        ),
        name="deconvolve",
    )(*[pltpu.with_memory_space_constraint(v, pltpu.HBM) for v in (psf_bank, ids, wts, ill_here, spread, moves, picks, observed, estimate, inv_all)])


def solution(mesh):
    placed = (
        P(None, "row", "col"),
        P(None, "row", "col"),
        P(("row", "col"), None, None, None, None),
        P("row", "col", None, None),
        P("row", "col", None, None),
        P(None, "row", "col"),
    )
    return jax.shard_map(
        functools.partial(shards, mesh.shape["row"], mesh.shape["col"]),
        mesh=mesh, in_specs=placed, out_specs=P(None, "row", "col"), check_vma=False,
    )
```

```python
import functools

import jax
import jax.numpy as jnp
import numpy as np
from jax import lax
from jax.experimental import pallas as pl
from jax.experimental.pallas import tpu as pltpu
from jax.sharding import PartitionSpec as P

MESH = pl.DeviceIdType.MESH
BF = jnp.bfloat16
F32 = jnp.float32
TAPS = 33
HALF = 16
GZ = 4
NT = (((1,), (1,)), ((), ()))


def mm(a, b):
    return jnp.dot(a, b, preferred_element_type=F32)


def mm_nt(a, b):
    return lax.dot_general(a, b, NT, preferred_element_type=F32)


def spread_table():
    w = np.zeros((128, 6 * 128), np.float32)
    for a in range(TAPS):
        plus, minus = (a - HALF) % 128, (HALF - a) % 128
        for lane in (a, TAPS + a):
            w[lane, minus] = 1.0
            w[lane, 128 + plus] = 1.0
            w[lane, 512:640] = 1.0
        w[2 * TAPS + a, 256 + plus] = 1.0
        w[2 * TAPS + a, 384 + minus] = 1.0
    w[3 * TAPS : 3 * TAPS + 3, 640:768] = 1.0
    return w.astype(BF)


def moves_table():
    eye = np.eye(128, dtype=np.float32)
    ends = np.concatenate([eye[:16], eye[112:]], 0)
    sel_r = np.zeros((GZ * 16, 128), np.float32)
    sel_l = np.zeros((GZ * 16, 128), np.float32)
    for zz in range(GZ):
        for i in range(16):
            sel_l[zz * 16 + i, zz * 32 + i] = 1.0
            sel_r[zz * 16 + i, zz * 32 + 16 + i] = 1.0
    none = np.zeros_like(sel_r)
    sel = np.block([[sel_r, none], [none, sel_l]])
    return np.concatenate([eye, ends], 0).astype(BF), sel.astype(BF)


def smoothing_table(length, n_row, rows):
    stiff = float(length * length) / 16.0
    d = np.diff(np.eye(length), axis=0)
    inv = np.linalg.inv(np.eye(length) + stiff * d.T @ d)
    rep = np.repeat(inv, rows * n_row // length, axis=1)
    return rep.reshape(length, n_row, rows).transpose(1, 0, 2).astype(np.float32)


def kernel(
    n_row, n_col, cells_hbm, ids_hbm, wts_hbm, ill_hbm, spread_hbm, moves_hbm, picks_hbm, obs_hbm, est_hbm, inv_all, out_hbm,
    cells, ids_in, wts_in, ill_in, spread, moves, picks,
    obs, est, out, wide, bank, ids, wts, ill_here, ext0, ext1, ext2, ext3, ystrip, strips, corn, cornsend, plane, ids_z, sel_send, sel_recv, ill, inv,
    base, rt0, rt1, ctc0, ctc1, ptc, cur, obs_t, rfac,
    in_sem, out_sem, psend, precv, isend, irecv, bsend, brecv, lsend, lrecv, hsend, hrecv,
):
    ext = (ext0, ext1, ext2, ext3)
    rt, ctc = (rt0, rt1), (ctc0, ctc1)
    depth = obs.shape[0]
    groups = depth // GZ
    planes = n_col // 4
    row = lax.axis_index("row")
    col = lax.axis_index("col")
    zc = col // 4
    slot = lax.rem(col, 4)
    core_col = zc * 4 + slot + 1 - 2 * lax.rem(slot, 2)
    x_col = zc * 4 + lax.rem(slot + 2, 4)

    def z_col(d):
        return lax.rem(zc + d + planes, planes) * 4 + slot

    up, down = lax.rem(row + n_row - 1, n_row), lax.rem(row + 1, n_row)
    left, right = lax.rem(col + n_col - 1, n_col), lax.rem(col + 1, n_col)

    barrier = pltpu.get_barrier_semaphore()
    friends = [(row, z_col(d)) for d in range(1, planes)]
    friends += [(row, core_col), (row, x_col), (row, zc * 4 + 3 - slot)]
    friends += [(lax.rem(row + d, n_row), col) for d in range(1, n_row)]
    friends += [(row, left), (row, right)]
    friends += [(up, left), (up, right), (down, left), (down, right)]
    for friend in friends:
        pl.semaphore_signal(barrier, inc=1, device_id=friend, device_id_type=MESH)

    small = [
        pltpu.make_async_copy(src, dst, in_sem.at[i])
        for i, (src, dst) in enumerate([
            (cells_hbm, cells), (ids_hbm, ids_in), (wts_hbm, wts_in), (ill_hbm, ill_in),
            (moves_hbm, moves), (est_hbm, est), (spread_hbm, spread), (picks_hbm, picks),
            (obs_hbm, obs), (inv_all.at[row], inv),
        ])
    ]
    for c in small:
        c.start()

    has = {"u": row > 0, "d": row < n_row - 1, "l": col > 0, "r": col < n_col - 1}

    def there(where):
        ok = has[where[0]]
        for w in where[1:]:
            ok = jnp.logical_and(ok, has[w])
        return ok

    def zero_unless(where, refs, *at):
        @pl.when(jnp.logical_not(there(where)))
        def _():
            for ref in refs:
                part = ref.at[at]
                part[...] = jnp.zeros(part.shape, BF)

    every, low_half, high_half = slice(None), slice(0, 16), slice(16, 32)
    zero_unless("r", ext, every, slice(128, 144), slice(0, 128))
    zero_unless("l", ext, every, slice(144, 160), slice(0, 128))
    zero_unless("d", [ystrip], every, every, low_half)
    zero_unless("u", [ystrip], every, every, high_half)
    zero_unless("dr", [corn], every, every, low_half, slice(0, 128))
    zero_unless("ur", [corn], every, every, high_half, slice(0, 128))
    zero_unless("dl", [corn], every, every, low_half, slice(128, 256))
    zero_unless("ul", [corn], every, every, high_half, slice(128, 256))

    for c in small[:4]:
        c.wait()
    zones = cells.shape[0]
    lane = lax.broadcasted_iota(jnp.int32, (16, 128), 1)
    quad = lax.broadcasted_iota(jnp.int32, (16, 128), 0)
    wide[...] = jnp.zeros_like(wide)
    for i in range(zones):
        for z in range(depth):
            at = (z % GZ) * 4
            for f in range(2):
                wide[f, i, z // GZ, at : at + 4, 0:TAPS] = cells[i, z, f]
    for i in range(zones):
        for g in range(groups):
            r, c = wide[0, i, g], wide[1, i, g]
            r_hi = r.astype(BF).astype(F32)
            total_c = jnp.sum(c, -1, keepdims=True)
            s_hi = total_c.astype(BF).astype(F32)
            s_mid = (total_c - s_hi).astype(BF).astype(F32)
            packed = r_hi + pltpu.roll(r - r_hi, TAPS, 1) + pltpu.roll(c, 2 * TAPS, 1)
            packed = jnp.where(lane == 3 * TAPS, s_hi, packed)
            packed = jnp.where(lane == 3 * TAPS + 1, s_mid, packed)
            packed = jnp.where(lane == 3 * TAPS + 2, total_c - s_hi - s_mid, packed)
            bank[g, i] = packed.astype(BF)
    tile_i = jnp.zeros((16, 128), F32)
    for g in range(groups):
        for k in range(2):
            lanes_here = lane // 16 == g * 2 + k
            tile_w = jnp.zeros((16, 128), F32)
            for zz in range(GZ):
                here = quad // 4 == zz
                both = jnp.logical_and(here, lanes_here)
                tile_i = jnp.where(both, ids_in[k, g * GZ + zz].astype(F32), tile_i)
                tile_w = jnp.where(here, wts_in[k, g * GZ + zz], tile_w)
            wts[g, k] = tile_w
    ids[...] = tile_i.astype(BF)
    ill_here[...] = jnp.zeros_like(ill_here)
    ill_here[:, 0 : ill_in.shape[1]] = ill_in[...]

    pl.semaphore_wait(barrier, len(friends))

    def remote(src, dst, s, r, to):
        return pltpu.make_async_remote_copy(
            src_ref=src, dst_ref=dst, send_sem=s, recv_sem=r, device_id=to, device_id_type=MESH
        )

    far_col = zc * 4 + 3 - slot

    def plane_copies(g):
        return [
            remote(bank.at[g], plane.at[g, slot], psend.at[g, i], precv.at[g, i], (row, to))
            for i, to in enumerate((x_col, far_col, core_col))
        ]

    def plane_start(g):
        for c in plane_copies(g):
            c.start()

    plane_start(0)
    id_copies = [
        remote(ids, ids_z.at[d], isend.at[d], irecv.at[d], (row, z_col(-d))) for d in range(1, planes)
    ]
    for c in id_copies:
        c.start()
    ill_copies = [
        remote(
            ill_here, ill.at[row], lsend.at[d], lrecv.at[d], (lax.rem(row + d, n_row), col)
        )
        for d in range(1, n_row)
    ]
    for g in range(groups):
        plane[g, slot] = bank[g]
    ids_z[0] = ids[...]
    ill[row] = ill_here[...]

    def halo_copies(p, g):
        zs = pl.ds(g * GZ, GZ)
        top, bottom = pl.ds(0, 16), pl.ds(16, 16)
        mid = pl.ds(0, 128)
        plan = [
            ("l", ext[p].at[zs, pl.ds(0, 16), mid], ext[p].at[zs, pl.ds(128, 16), mid], (row, left)),
            ("r", ext[p].at[zs, pl.ds(112, 16), mid], ext[p].at[zs, pl.ds(144, 16), mid], (row, right)),
            ("u", strips.at[p, zs, top], ystrip.at[p, zs, top], (up, col)),
            ("d", strips.at[p, zs, bottom], ystrip.at[p, zs, bottom], (down, col)),
            ("ul", cornsend.at[p, g, top], corn.at[p, g, top, pl.ds(0, 128)], (up, left)),
            ("dl", cornsend.at[p, g, bottom], corn.at[p, g, bottom, pl.ds(0, 128)], (down, left)),
            ("ur", cornsend.at[p, g, top], corn.at[p, g, top, pl.ds(128, 128)], (up, right)),
            ("dr", cornsend.at[p, g, bottom], corn.at[p, g, bottom, pl.ds(128, 128)], (down, right)),
        ]
        return [
            (where, remote(src, dst, hsend.at[p, g, i], hrecv.at[p, g, i], to))
            for i, (where, src, dst, to) in enumerate(plan)
        ]

    opposite = {"u": "d", "d": "u", "l": "r", "r": "l"}

    def halo_start(p, g):
        for where, c in halo_copies(p, g):
            @pl.when(there(where))
            def _():
                c.start()

    def halo_wait_recv(p, g):
        for where, c in halo_copies(p, g):
            @pl.when(there("".join(opposite[w] for w in where)))
            def _():
                c.wait_recv()

    def halo_wait_send(p, g):
        for where, c in halo_copies(p, g):
            @pl.when(there(where))
            def _():
                c.wait_send()

    quarter = lax.broadcasted_iota(jnp.int32, (32, 128), 1) // 32

    def pack(p, g, fields):
        for zz in range(GZ):
            ext[p][g * GZ + zz, 0:128, 0:128] = fields[zz]
        s = mm_nt(moves[128:160], jnp.concatenate(fields, 0)).astype(BF)
        for zz in range(GZ):
            strips[p, g * GZ + zz] = s[:, zz * 128 : (zz + 1) * 128]
        c = jnp.zeros((32, 128), F32)
        for zz in range(GZ):
            turned = pltpu.roll(s[:, zz * 128 : (zz + 1) * 128].astype(F32), 16 + zz * 32, 1)
            c = jnp.where(quarter == zz, turned, c)
        cornsend[p, g] = c.astype(BF)
        halo_start(p, g)

    def first_field(g):
        fields = []
        for zz in range(GZ):
            z = g * GZ + zz
            c = jnp.transpose(est[z])
            cur[z] = c
            fields.append(c.astype(BF))
        pack(0, g, fields)

    for c in small[4:6]:
        c.wait()
    for g in range(groups):
        if g:
            plane_start(g)
        first_field(g)
    for c in ill_copies:
        c.start()

    for c in id_copies:
        c.wait_recv()

    def sel_copy(g, d):
        return remote(
            sel_send.at[g, d], sel_recv.at[g, d], bsend.at[g, d], brecv.at[g, d], (row, z_col(d))
        )

    def select(g):
        for c in plane_copies(g):
            c.wait_recv()
        for d in range(planes):
            for k in range(2):
                one = jnp.where(lane == (g * 2 + k) * 16, ids_z[d].astype(F32), 0.0)
                mine = jnp.broadcast_to(jnp.sum(one, -1, keepdims=True), (16, 128))
                picked = jnp.zeros((16, 128), F32)
                for s in range(4):
                    for i in range(4):
                        zone = (zc * 16 + s * 4 + i).astype(F32)
                        picked = jnp.where(mine == zone, plane[g, s, i].astype(F32), picked)
                sel_send[g, d, k] = picked.astype(BF)
        for d in range(1, planes):
            sel_copy(g, d).start()

    pl.loop(0, 4)(select)

    for c in small[6:]:
        c.wait()

    def smooth():
        for c in ill_copies:
            c.wait_recv()
        coarse = ill_in.shape[1]
        fac = jnp.zeros((depth, inv.shape[1]), F32)
        for i in range(n_row):
            fac = fac + jnp.dot(
                ill[i, :, 0:coarse], inv[i * coarse : (i + 1) * coarse],
                precision=lax.Precision.HIGHEST, preferred_element_type=F32,
            )
        rfac[...] = 1.0 / fac

    def spread_taps(g):
        for d in range(1, planes):
            sel_copy(g, d).wait_recv()

        picked = sel_send[g, 0].astype(F32)
        for d in range(1, planes):
            picked = picked + sel_recv[g, d].astype(F32)
        b = mm(jnp.reshape(picked, (32, 128)).astype(BF), spread[...])
        r = (b[0:16], b[16:32])
        total = wts[g, 0] * r[0][:, 512:640] * r[0][:, 640:768]
        total = total + wts[g, 1] * r[1][:, 512:640] * r[1][:, 640:768]
        for shift in (1, 2):
            even = (quad // shift) % 2 == 0
            total = total + jnp.where(even, pltpu.roll(total, 16 - shift, 0), pltpu.roll(total, shift, 0))
        for k in range(2):
            for t in range(4):
                v = r[k][:, t * 128 : (t + 1) * 128]
                base[t, g, k] = (wts[g, k] * v) / total if t < 2 else v

    low = lax.broadcasted_iota(jnp.int32, (16, 128), 1) < 64
    lower = low.astype(F32).astype(BF)
    upper = 1.0 - lower

    def circulant(t, j, g, zz):
        b = jnp.broadcast_to(base[t, g, j // 4, pl.ds(zz * 4 + j % 4, 1), :], (16, 128))
        b = pltpu.roll(b, 0, 1, stride=1, stride_axis=0).astype(BF)
        return [pltpu.roll(b, 16 * i, 1) if i else b for i in range(8)]

    def build(way, g, zz):
        z = g * GZ + zz
        left_h = [0.0, 0.0]
        right_h = [0.0, 0.0]
        for j in range(8):
            js = slice(j * 128, (j + 1) * 128)
            r = circulant(way, j, g, zz)
            c = circulant(2 + way, j, g, zz)
            for i in range(1, 7):
                rt[way][z, i * 16 : i * 16 + 16, js] = r[i]
                ctc[way][z, i * 16 : i * 16 + 16, js] = c[i]
            rt[way][z, 0:16, js] = r[0] * lower
            rt[way][z, 112:128, js] = r[7] * upper
            rt[way][z, 128:144, js] = r[0] * upper
            rt[way][z, 144:160, js] = r[7] * lower
            ctc[way][z, 0:16, js] = c[0] * lower
            ctc[way][z, 112:128, js] = c[7] * upper
            at = (j % 4) * 32
            left_h[j // 4] += pltpu.roll(c[0] * upper, (at + 16 + 16) % 128, 1)
            right_h[j // 4] += pltpu.roll(c[7] * lower, at, 1) if at else c[7] * lower
        for h in range(2):
            hs = slice(1024 + h * 128, 1152 + h * 128)
            ctc[way][z, 0:16, hs] = left_h[h]
            ctc[way][z, 16:112, hs] = jnp.zeros((96, 128), BF)
            ctc[way][z, 112:128, hs] = right_h[h]

    def out_copy(g):
        zs = pl.ds(g * GZ, GZ)
        return pltpu.make_async_copy(out.at[zs], out_hbm.at[zs], out_sem.at[g])

    def unpack(p, g):
        edges = jnp.reshape(ystrip[p, pl.ds(g * GZ, GZ)], (GZ * 32, 128))
        mid = mm_nt(moves[0:128], edges)
        corner = mm_nt(picks[...], corn[p, g]).astype(BF)
        for zz in range(GZ):
            z = g * GZ + zz
            turned = pltpu.roll(mid, 128 - zz * 32, 1) if zz else mid
            ext[p][z, 0:128, 128:160] = turned[:, 0:32].astype(BF)
            at = zz * 16
            ext[p][z, 128:144, 128:160] = corner[at : at + 16]
            at = (GZ + zz) * 16
            ext[p][z, 144:160, 128:160] = corner[at : at + 16]

    def rows_stage(p, z, zz):
        field = ext[p][z, :, 0:160]
        for jp in range(4):
            o = mm(field, rt[p % 2][z, :, jp * 256 : (jp + 1) * 256]).astype(BF)
            for h in range(2):
                j = jp * 2 + h
                ptc[zz, j * 128 : (j + 1) * 128] = o[0:128, h * 128 : (h + 1) * 128]
                ptc[zz, 1024 + j * 32 : 1056 + j * 32] = o[128:160, h * 128 : (h + 1) * 128]

    def cols_stage(p, z, zz):
        return mm(ctc[p % 2][z], ptc[zz])

    for p in range(4):
        if p == 1:
            smooth()

        @pl.loop(0, groups)
        def _(g):
            if p == 0:
                spread_taps(g)
            if p < 2:
                @pl.loop(0, GZ)
                def _(zz):
                    build(p, g, zz)
            halo_wait_recv(p, g)
            unpack(p, g)
            fields = []
            for step in range(GZ + 1):
                if step < GZ:
                    rows_stage(p, g * GZ + step, step)
                if step == 0:
                    continue
                zz = step - 1
                z = g * GZ + zz
                f = cols_stage(p, z, zz)
                if p % 2 == 0:
                    fields.append((jnp.transpose(obs[z]) / f if p == 0 else obs_t[z] / f).astype(BF))
                    if p == 0:
                        obs_t[z] = jnp.transpose(obs[z])
                else:
                    new = cur[z] * f * rfac[pl.ds(z, 1), :]
                    if p == 3:
                        out[z] = jnp.transpose(new)
                    else:
                        cur[z] = new
                        fields.append(new.astype(BF))
            if p < 3:
                pack(p + 1, g, fields)
            else:
                out_copy(g).start()

    for g in range(groups):
        for c in plane_copies(g):
            c.wait_send()
    for c in id_copies + ill_copies:
        c.wait_send()
    @pl.loop(0, groups)
    def _(g):
        for d in range(1, planes):
            sel_copy(g, d).wait_send()

    for g in range(groups):
        out_copy(g).wait()
    for p in range(4):
        @pl.loop(0, groups)
        def _(g):
            halo_wait_send(p, g)


def shards(n_row, n_col, observed, estimate, psf_bank, zone_ids, mix_weights, illumination):
    depth, rows, cols = estimate.shape
    zones = psf_bank.shape[0]
    groups = depth // GZ
    planes = n_col // 4
    ids = zone_ids[0, 0].T
    wts = mix_weights[0, 0].T
    ill_here = illumination[:, :, 0]
    length = illumination.shape[1] * n_row
    spread = jnp.asarray(spread_table())
    moves, picks = map(jnp.asarray, moves_table())
    inv_all = jnp.asarray(smoothing_table(length, n_row, rows))
    hbm = pl.BlockSpec(memory_space=pl.ANY)
    dma = pltpu.SemaphoreType.DMA
    return pl.pallas_call(
        functools.partial(kernel, n_row, n_col),
        out_shape=jax.ShapeDtypeStruct(estimate.shape, F32),
        in_specs=[hbm] * 10,
        out_specs=pl.BlockSpec(memory_space=pl.ANY),
        scratch_shapes=[
            pltpu.VMEM(psf_bank.shape, F32),
            pltpu.SMEM(ids.shape, jnp.int32),
            pltpu.SMEM(wts.shape, F32),
            pltpu.VMEM(ill_here.shape, F32),
            pltpu.VMEM(spread.shape, BF),
            pltpu.VMEM(moves.shape, BF),
            pltpu.VMEM(picks.shape, BF),
            *[pltpu.VMEM((depth, rows, cols), F32)] * 3,
            pltpu.VMEM((2, zones, groups, 16, 128), F32),
            pltpu.VMEM((groups, zones, 16, 128), BF),
            pltpu.VMEM((16, 128), BF),
            pltpu.VMEM((groups, 2, 16, 128), F32),
            pltpu.VMEM((depth, 128), F32),
            *[pltpu.VMEM((depth, 160, 256), BF)] * 4,
            pltpu.VMEM((4, depth, 32, 128), BF),
            pltpu.VMEM((4, depth, 32, 128), BF),
            pltpu.VMEM((4, groups, 32, 256), BF),
            pltpu.VMEM((4, groups, 32, 128), BF),
            pltpu.VMEM((groups, 4, zones, 16, 128), BF),
            pltpu.VMEM((planes, 16, 128), BF),
            pltpu.VMEM((groups, planes, 2, 16, 128), BF),
            pltpu.VMEM((groups, planes, 2, 16, 128), BF),
            pltpu.VMEM((n_row, depth, 128), F32),
            pltpu.VMEM((length, rows), F32),
            pltpu.VMEM((4, groups, 2, 16, 128), F32),
            *[pltpu.VMEM((depth, 160, 1024), BF)] * 2,
            *[pltpu.VMEM((depth, 128, 1280), BF)] * 2,
            pltpu.VMEM((GZ, 1280, 128), BF),
            pltpu.VMEM((depth, 128, 128), F32),
            pltpu.VMEM((depth, 128, 128), F32),
            pltpu.VMEM((depth, 128), F32),
            dma((10,)), dma((groups,)),
            dma((groups, 3)), dma((groups, 3)),
            dma((planes,)), dma((planes,)),
            dma((groups, planes)), dma((groups, planes)),
            dma((n_row,)), dma((n_row,)),
            dma((4, groups, 8)), dma((4, groups, 8)),
        ],
        compiler_params=pltpu.CompilerParams(
            collective_id=0, has_side_effects=True, vmem_limit_bytes=44 * 2**20
        ),
        name="deconvolve",
    )(*[pltpu.with_memory_space_constraint(v, pltpu.HBM) for v in (psf_bank, ids, wts, ill_here, spread, moves, picks, observed, estimate, inv_all)])


def solution(mesh):
    placed = (
        P(None, "row", "col"),
        P(None, "row", "col"),
        P(("row", "col"), None, None, None, None),
        P("row", "col", None, None),
        P("row", "col", None, None),
        P(None, "row", "col"),
    )
    return jax.shard_map(
        functools.partial(shards, mesh.shape["row"], mesh.shape["col"]),
        mesh=mesh, in_specs=placed, out_specs=P(None, "row", "col"), check_vma=False,
    )
```
